256 devices in a mesh: grp: 8 (over y, core), tbl: 32 (over z, x).
Axes of the slice: x: 4, y: 4, z: 8, core: 2. Of those that a mesh axis runs over, the one named last changes fastest.
Arguments:
- user_feats: bfloat16 [4096, 128], P(('grp', 'tbl')), may hold values from -6 to 6
- tower_in: bfloat16 [128, 4096], replicated, may hold values from -0.5 to 0.5
- tower_out: bfloat16 [4096, 256], replicated, may hold values from -0.09375 to 0.09375
- table: bfloat16 [8192, 256], P('tbl'), may hold values from -3 to 3
- inter_weight: bfloat16 [256, 512], replicated, may hold values from -0.375 to 0.375
- out_weight: float32 [512], replicated, may hold values from -0.3 to 0.3
- ids: int32 [256, 32, 4, 32], P(('grp', 'tbl')), may hold values from 0 to 255
- live: int32 [256, 32], P(('grp', 'tbl')), may hold values from 1 to 32, as said below
- req_of: int32 [256, 32, 32], P(('grp', 'tbl')), may hold values from 0 to 511
- labels: float32 [256, 32, 32], P(('grp', 'tbl')), may hold values from 0 to 1
Outputs:
- scores: float32 [256, 32, 32], P(('grp', 'tbl'))
- grad_tower_in: float32 [128, 4096], replicated
- grad_tower_out: float32 [4096, 256], replicated
- grad_inter: float32 [256, 512], replicated
- grad_out: float32 [512], replicated
- grad_table: float32 [8192, 256], P('tbl')
The draws below stay inside these ranges and needn't reach their ends.
Inputs may be any that keep to these rules, and one draw needn't show every extreme that they name: In every draw, in each group, some device gets 32 live slots from every owner; the others get between 1 and 32 live slots from each owner.
All inputs are finite; a program needn't handle non-finite values.
Results may differ from the reference program's by a relative error of at most 0.0067.
Values may be sent and summed in bfloat16 or wider, within the bound.
No kernel may reach another device: no remote copies, remote signals or barrier semaphores. Data moves between devices by JAX's collectives and lax.ppermute only.
A program may use at most 64 MiB of HBM per device.

```python
import math
import jax
import jax.numpy as jnp
import numpy as np
from jax import lax

UF = 128
H = 4096
E = 256
HI = 512
BAG = 4
SLOT = 32
TROWS_DEV = 256
REQ_GRP = 512
N_GRP = 8
N_TBL = 32


def draw_live(key, part):
    base_key = jax.random.fold_in(key, 11)
    first, second, third = jax.random.split(base_key, 3)
    factor = jax.random.randint(first, (N_GRP, 1, N_TBL), 1, 5)
    base = jax.random.randint(second, (N_GRP, N_TBL, N_TBL), 0, SLOT)
    counts = 1 + base * factor // 4
    full = jax.random.randint(third, (N_GRP, 1, 1), 0, N_TBL)
    dest = jnp.arange(N_TBL, dtype=jnp.int32)[None, :, None]
    counts = jnp.where(dest == full, SLOT, counts)
    return counts.reshape(N_GRP * N_TBL, N_TBL).astype(jnp.int32)


def touch_ends(drawn, own_key, least, largest):
    place = [jax.random.randint(jax.random.fold_in(own_key, axis), (), 0, length) for axis, length in enumerate(drawn.shape)]
    longest = drawn.shape.index(max(drawn.shape))
    next_to = place[:longest] + [(place[longest] + 1) % drawn.shape[longest]] + place[longest + 1:]
    return drawn.at[tuple(place)].set(least).at[tuple(next_to)].set(largest)


def block_scale(rng, dims, pieces, least, top_value):
    def one(position, parts):
        steps = jax.random.uniform(jax.random.fold_in(jax.random.fold_in(rng, 6), position), (parts,), jnp.float32, least / len(pieces), top_value / len(pieces))
        return jnp.repeat(jnp.exp(steps), dims[position] // parts).reshape((-1,) + (1,) * (len(dims) - position - 1))

    level = one(*pieces[0])
    for cut in pieces[1:]:
        level = level * one(*cut)
    return level


def rank_bounds(count, lean):
    weights = [(1 << 20) // math.isqrt(rank ** lean) + 1 for rank in range(1, count + 1)]
    scale = 1 + sum(weights) // (1 << 30)
    return np.cumsum(np.array([max(1, weight // scale) for weight in weights]))


def ranked_ids(stream_key, extent, number_of, slope):
    grid = rank_bounds(number_of, slope)
    lot = jax.random.randint(jax.random.fold_in(stream_key, 1), extent, 0, int(grid[number_of - 1]))
    standing = jnp.searchsorted(jnp.asarray(grid, jnp.int32), lot, side="right")
    return jax.random.permutation(jax.random.fold_in(stream_key, 2), number_of)[standing].astype(jnp.int32)


def noise(stream_key, dims, scale, limit, shards=(), held_as=jnp.bfloat16):
    entries = scale * jax.random.normal(stream_key, dims, jnp.float32)
    if shards:
        entries = entries * block_scale(stream_key, dims, shards, -0.22, 0.18)
    return jnp.clip(entries, -limit, limit).astype(held_as)


def setup_inputs(seed: int = 0) -> dict:
    key_of = jax.random.split(jax.random.key(seed), 11)
    user_feats = noise(key_of[0], (N_GRP * REQ_GRP, UF), 1.0, 6.0, ((0, 256),))
    tower_in = noise(key_of[1], (UF, H), UF ** -0.5, 0.5)
    tower_out = noise(key_of[2], (H, E), H ** -0.5, 0.09375)
    table = noise(key_of[3], (N_TBL * TROWS_DEV, E), 0.5, 3.0, ((0, 32),))
    inter_weight = noise(key_of[4], (E, HI), E ** -0.5, 0.375)
    out_weight = noise(key_of[5], (HI,), 0.05, 0.3, (), jnp.float32)
    ids = touch_ends(jax.random.randint(key_of[6], (N_GRP * N_TBL, N_TBL, BAG, SLOT), 0, TROWS_DEV), jax.random.fold_in(key_of[6], 1), 0, TROWS_DEV - 1).astype(jnp.int32)
    live = draw_live(jax.random.fold_in(key_of[10], 71), 0)
    req_of = touch_ends(ranked_ids(key_of[8], (N_GRP * N_TBL, N_TBL, SLOT), REQ_GRP, 2), jax.random.fold_in(key_of[8], 3), 0, REQ_GRP - 1).astype(jnp.int32)
    labels = jnp.clip(1.0 * jax.random.uniform(key_of[9], (N_GRP * N_TBL, N_TBL, SLOT), jnp.float32) ** block_scale(key_of[9], (N_GRP * N_TBL, N_TBL, SLOT), ((0, 256),), -0.2, 0.2), 0.0, 1.0)
    return dict(user_feats=user_feats, tower_in=tower_in, tower_out=tower_out, table=table, inter_weight=inter_weight, out_weight=out_weight, ids=ids, live=live, req_of=req_of, labels=labels)


def silu_slope(value):
    sig = jax.nn.sigmoid(value)
    return sig * (1.0 + value * (1.0 - sig))

def reference(user_feats, tower_in, tower_out, table, inter_weight, out_weight, ids, live, req_of, labels):
    highest = lax.Precision.HIGHEST
    pre = jnp.dot(user_feats, tower_in, preferred_element_type=jnp.float32)
    hidden = jax.nn.silu(pre).astype(jnp.bfloat16)
    users = jnp.dot(hidden, tower_out, preferred_element_type=jnp.float32).astype(jnp.bfloat16)
    factor = 1.0 / math.sqrt(N_GRP * N_TBL * N_TBL * SLOT)
    offset = (jnp.arange(N_TBL, dtype=jnp.int32) * TROWS_DEV)[:, None, None]
    slot_index = jnp.arange(SLOT, dtype=jnp.int32)
    grad_inter = jnp.zeros((E, HI), jnp.float32)
    grad_out = jnp.zeros((HI,), jnp.float32)
    grad_table = jnp.zeros((N_TBL * TROWS_DEV, E), jnp.float32)
    score_list = []
    duser_list = []
    for group in range(N_GRP):
        lo = group * N_TBL
        group_ids = ids[lo:lo + N_TBL]
        summed = jnp.zeros((N_TBL, N_TBL, SLOT, E), jnp.float32)
        for bag in range(BAG):
            summed = summed + table[group_ids[:, :, bag, :] + offset].astype(jnp.float32)
        pooled = summed.astype(jnp.bfloat16)
        items = jnp.transpose(pooled, (1, 0, 2, 3)).reshape(-1, E)
        request = req_of[lo:lo + N_TBL].reshape(-1).astype(jnp.int32)
        group_users = users[group * REQ_GRP:(group + 1) * REQ_GRP]
        chosen = group_users[request]
        cross = (items.astype(jnp.float32) * chosen.astype(jnp.float32)).astype(jnp.bfloat16)
        inner = jnp.dot(cross, inter_weight, preferred_element_type=jnp.float32)
        act = jax.nn.silu(inner)
        score = lax.optimization_barrier(jnp.sum(act * out_weight, axis=1))
        mask = (slot_index[None, None, :] < live[lo:lo + N_TBL][:, :, None]).reshape(-1)
        target = labels[lo:lo + N_TBL].reshape(-1)
        grad_score = jnp.where(mask, jax.nn.sigmoid(score) - target, 0.0) * factor
        dinner = (grad_score[:, None] * out_weight * silu_slope(inner)).astype(jnp.bfloat16)
        grad_inter = grad_inter + jnp.dot(cross.T, dinner, preferred_element_type=jnp.float32)
        grad_out = grad_out + lax.optimization_barrier(jnp.sum(grad_score[:, None] * act, axis=0))
        dcross = jnp.dot(dinner, inter_weight.T, preferred_element_type=jnp.float32)
        d_item = dcross * chosen.astype(jnp.float32)
        d_user = dcross * items.astype(jnp.float32)
        duser_list.append(jax.ops.segment_sum(d_user, request, num_segments=REQ_GRP))
        back = jnp.transpose(d_item.reshape(N_TBL, N_TBL, SLOT, E), (1, 0, 2, 3)).reshape(-1, E)
        for bag in range(BAG):
            where_rows = (group_ids[:, :, bag, :] + offset).reshape(-1).astype(jnp.int32)
            grad_table = grad_table + jax.ops.segment_sum(back, where_rows, num_segments=N_TBL * TROWS_DEV)
        score_list.append(score.reshape(N_TBL, N_TBL, SLOT))
    d_users = jnp.concatenate(duser_list, axis=0)
    grad_tower_out = jnp.dot(hidden.astype(jnp.float32).T, d_users, precision=highest)
    d_hidden = jnp.dot(d_users, tower_out.astype(jnp.float32).T, precision=highest)
    d_pre = d_hidden * silu_slope(pre)
    grad_tower_in = jnp.dot(user_feats.astype(jnp.float32).T, d_pre, precision=highest)
    scores = jnp.concatenate(score_list, axis=0)
    return (scores, grad_tower_in, grad_tower_out, grad_inter, grad_out, grad_table)
```

```python
import math

import jax
import jax.numpy as jnp
from jax import lax
from jax.experimental import pallas as pl
from jax.experimental.pallas import tpu as pltpu
from jax.sharding import PartitionSpec as P

BF = jnp.bfloat16
F32 = jnp.float32


def to_bf(value):
    return lax.reduce_precision(value, 8, 7)


def mm(a, b):
    return jnp.dot(a, b, preferred_element_type=F32)


def mm_nt(a, b):
    return lax.dot_general(a, b, (((1,), (1,)), ((), ())), preferred_element_type=F32)


def slope_of(value, sig):
    return sig * (1.0 + value * (1.0 - sig))


def pool_kernel(ids_ref, table_ref, items_ref, counts_ref):
    rows, cands = counts_ref.shape
    row = lax.broadcasted_iota(jnp.int32, (rows, cands), 0)
    total = jnp.zeros((rows, cands), F32)
    for b in range(ids_ref.shape[0]):
        total = total + jnp.where(row == ids_ref[b : b + 1, :], 1.0, 0.0)
    counts = total.astype(BF)
    counts_ref[...] = counts
    items_ref[...] = mm(table_ref[...].astype(F32).T.astype(BF), counts).astype(BF)


def pool(ids, table):
    cands = ids.shape[1]
    rows, width = table.shape
    return pl.pallas_call(
        pool_kernel,
        out_shape=(
            jax.ShapeDtypeStruct((width, cands), BF),
            jax.ShapeDtypeStruct((rows, cands), BF),
        ),
        compiler_params=pltpu.CompilerParams(vmem_limit_bytes=16 << 20),
        cost_estimate=pl.CostEstimate(
            flops=2 * cands * rows * width, bytes_accessed=2 << 20, transcendentals=0
        ),
        name="pool",
    )(ids, table)


def tower_kernel(feats_ref, win_ref, wout_ref, hid_ref, slope_ref, users_ref, acc):
    step = pl.program_id(0)
    pre = mm(feats_ref[...], win_ref[...])
    sig = jax.nn.sigmoid(pre)
    hidden = pre * sig
    slope_ref[...] = slope_of(pre, sig).astype(BF)
    hidden_bf = hidden.astype(BF)
    hid_ref[...] = hidden.T.astype(BF)
    part = mm(hidden_bf, wout_ref[...])

    @pl.when(step == 0)
    def _():
        acc[...] = part

    @pl.when(step > 0)
    def _():
        acc[...] += part

    @pl.when(step == pl.num_programs(0) - 1)
    def _():
        users_ref[...] = acc[...].T.astype(BF)


def side_tower_kernel(feats_ref, win_ref, hid_ref, slope_ref):
    pre = mm(feats_ref[...], win_ref[...])
    sig = jax.nn.sigmoid(pre)
    slope_ref[...] = slope_of(pre, sig).astype(BF)
    hid_ref[...] = (pre * sig).T.astype(BF)


def tower(feats, tower_in, tower_out, with_users):
    reqs, uf = feats.shape
    wide, width = tower_out.shape
    block = 512
    hid = jax.ShapeDtypeStruct((wide, reqs), BF)
    slope = jax.ShapeDtypeStruct((reqs, wide), BF)
    hid_spec = pl.BlockSpec((block, reqs), lambda i: (i, 0))
    slope_spec = pl.BlockSpec((reqs, block), lambda i: (0, i))
    ins = [pl.BlockSpec((reqs, uf), lambda i: (0, 0)), pl.BlockSpec((uf, block), lambda i: (0, i))]
    cost = pl.CostEstimate(
        flops=2 * reqs * wide * (uf + (width if with_users else 0)),
        bytes_accessed=10 << 20,
        transcendentals=reqs * wide,
    )
    params = pltpu.CompilerParams(vmem_limit_bytes=32 << 20)
    if with_users:
        return pl.pallas_call(
            tower_kernel,
            grid=(wide // block,),
            in_specs=ins + [pl.BlockSpec((block, width), lambda i: (i, 0))],
            out_specs=(hid_spec, slope_spec, pl.BlockSpec((width, reqs), lambda i: (0, 0))),
            out_shape=(hid, slope, jax.ShapeDtypeStruct((width, reqs), BF)),
            scratch_shapes=[pltpu.VMEM((reqs, width), F32)],
            compiler_params=params,
            cost_estimate=cost,
            name="tower",
        )(feats, tower_in, tower_out)
    return pl.pallas_call(
        side_tower_kernel,
        grid=(wide // block,),
        in_specs=ins,
        out_specs=(hid_spec, slope_spec),
        out_shape=(hid, slope),
        compiler_params=params,
        cost_estimate=cost,
        name="side_tower",
    )(feats, tower_in)


def rank_kernel(
    factor, slots, users_ref, items_ref, counts_ref, meta_ref, iw_ref, w_ref,
    score_ref, sent_ref, gt_ref, acc_u, acc_g, acc_t, acc_o,
):
    cands = items_ref.shape[1]
    reqs = users_ref.shape[1]
    width, hi_units = iw_ref.shape
    step_c = 256
    iw = iw_ref[...]
    iw_t = iw.astype(F32).T.astype(BF)
    weight = w_ref[...]
    users = users_ref[...]
    for k in range(cands // step_c):
        cut = slice(k * step_c, (k + 1) * step_c)
        meta = meta_ref[:, cut].astype(F32)
        request = (meta[0:1] * 16.0 + meta[1:2]).astype(jnp.int32)
        target = meta[2:3] + meta[3:4] + meta[4:5]
        live = meta[5:6]
        slot = lax.broadcasted_iota(jnp.int32, (1, step_c), 1) % slots
        row = lax.broadcasted_iota(jnp.int32, (reqs, step_c), 0)
        pick = jnp.where(row == request, 1.0, 0.0).astype(BF)
        chosen = mm(users, pick)
        item = items_ref[:, cut].astype(F32)
        cross = (item * chosen).astype(BF)
        inner = mm(iw_t, cross)
        sig = jax.nn.sigmoid(inner)
        act = inner * sig
        score = jnp.sum(act * weight, axis=0, keepdims=True)
        score_ref[:, cut] = score
        grad = jnp.where(slot.astype(F32) < live, jax.nn.sigmoid(score) - target, 0.0) * factor
        dz = (grad * weight * slope_of(inner, sig)).astype(BF)
        dcross = mm(iw, dz)
        d_item = (dcross * chosen).astype(BF)
        d_user = (dcross * item).astype(BF)
        terms = mm_nt(pick, d_user)
        g_in = mm_nt(cross, dz)
        g_t = mm_nt(counts_ref[:, cut], d_item)
        g_o = mm_nt(jnp.broadcast_to(grad, (8, step_c)), act)
        if k == 0:
            acc_u[...] = terms
            acc_g[...] = g_in
            acc_t[...] = g_t
            acc_o[...] = g_o
        else:
            acc_u[...] += terms
            acc_g[...] += g_in
            acc_t[...] += g_t
            acc_o[...] += g_o
    shards = sent_ref.shape[0]
    each = reqs // shards
    sent_ref[:, 0:each, :] = acc_u[...].astype(BF).reshape(shards, each, width)
    half = shards // 2
    sent_ref[0:half, each : 2 * each, :] = acc_g[:, 0:width].astype(BF).reshape(half, each, width)
    sent_ref[half:, each : 2 * each, :] = acc_g[:, width:].astype(BF).reshape(half, each, width)
    out = acc_o[...].astype(BF)
    tail = jnp.concatenate([out[0:1, 0:width], out[0:1, width:]], axis=0)
    sent_ref[:, 2 * each : 2 * each + 2, :] = jnp.broadcast_to(tail[None], (shards, 2, width))
    gt_ref[...] = acc_t[...].astype(BF)


def rank(factor, slots, shards, users, items, counts, meta, iw, weight):
    width, cands = items.shape
    reqs = users.shape[1]
    hi_units = iw.shape[1]
    rows = counts.shape[0]
    each = reqs // shards
    return pl.pallas_call(
        lambda *refs: rank_kernel(factor, slots, *refs),
        out_shape=(
            jax.ShapeDtypeStruct((1, cands), F32),
            jax.ShapeDtypeStruct((shards, 2 * each + 2, width), BF),
            jax.ShapeDtypeStruct((rows, width), BF),
        ),
        scratch_shapes=[
            pltpu.VMEM((reqs, width), F32),
            pltpu.VMEM((width, hi_units), F32),
            pltpu.VMEM((rows, width), F32),
            pltpu.VMEM((8, hi_units), F32),
        ],
        compiler_params=pltpu.CompilerParams(vmem_limit_bytes=32 << 20),
        cost_estimate=pl.CostEstimate(
            flops=2 * cands * width * (reqs * 2 + hi_units * 3 + rows),
            bytes_accessed=4 << 20,
            transcendentals=cands * hi_units,
        ),
        name="rank",
    )(users, items, counts, meta, iw, weight)


def dense_kernel(*refs):
    d, ft, hid, slope = refs[0:4], refs[4:8], refs[8:12], refs[12:16]
    wout_ref, gout_ref, gin_ref = refs[16], refs[17], refs[18]
    wout = wout_ref[...]
    outs, ins = [], []
    for k in range(4):
        d_k = d[k][...]
        outs.append(mm(hid[k][...], d_k))
        d_pre = (mm_nt(d_k, wout) * slope[k][...].astype(F32)).astype(BF)
        ins.append(mm(ft[k][...], d_pre))
    gout_ref[...] = ((outs[0] + outs[3]) + (outs[1] + outs[2])).astype(BF)
    gin_ref[...] = ((ins[0] + ins[3]) + (ins[1] + ins[2])).astype(BF)


def dense(d, ft, hid, slope, tower_out):
    wide, width = tower_out.shape
    reqs = d[0].shape[0]
    uf = ft[0].shape[0]
    block = 512
    return pl.pallas_call(
        dense_kernel,
        grid=(wide // block,),
        in_specs=[pl.BlockSpec((reqs, width), lambda i: (0, 0))] * 4
        + [pl.BlockSpec((uf, reqs), lambda i: (0, 0))] * 4
        + [pl.BlockSpec((block, reqs), lambda i: (i, 0))] * 4
        + [pl.BlockSpec((reqs, block), lambda i: (0, i))] * 4
        + [pl.BlockSpec((block, width), lambda i: (i, 0))],
        out_specs=(
            pl.BlockSpec((block, width), lambda i: (i, 0)),
            pl.BlockSpec((uf, block), lambda i: (0, i)),
        ),
        out_shape=(
            jax.ShapeDtypeStruct((wide, width), BF),
            jax.ShapeDtypeStruct((uf, wide), BF),
        ),
        compiler_params=pltpu.CompilerParams(vmem_limit_bytes=40 << 20),
        cost_estimate=pl.CostEstimate(
            flops=8 * reqs * wide * (2 * width + uf), bytes_accessed=40 << 20, transcendentals=0
        ),
        name="dense",
    )(*d, *ft, *hid, *slope, tower_out)


def body(
    user_feats, tower_in, tower_out, table, inter_weight, out_weight, ids, live, req_of, labels
):
    groups = lax.axis_size("grp")
    shards = lax.axis_size("tbl")
    slots = ids.shape[3]
    width = table.shape[1]
    each = user_feats.shape[0]
    uf = user_feats.shape[1]
    reqs = each * shards
    chips = groups // 2

    def ring(turn, other):
        return [
            (y * 2 + c, ((y + turn) % chips) * 2 + (c + other) % 2)
            for y in range(chips)
            for c in range(2)
        ]

    def from_chips(x):
        return [lax.ppermute(x, "grp", ring(turn, 0)) for turn in (1, chips - 1, 2)]

    def swap(x):
        return lax.ppermute(x, "grp", ring(0, 1))

    def group_sum(x):
        pair = (x.astype(F32) + swap(x).astype(F32)).astype(BF)
        a, b, c = from_chips(pair)
        return (pair.astype(F32) + c.astype(F32)) + (a.astype(F32) + b.astype(F32))

    def exchange(x):
        return lax.all_to_all(x, "tbl", split_axis=0, concat_axis=0, tiled=True)

    request = req_of[0]
    req_hi = request // 16
    req_lo = request - req_hi * 16
    lab = labels[0]
    lab_hi = to_bf(lab)
    lab_mid = to_bf(lab - lab_hi)
    lab_lo = lab - lab_hi - lab_mid
    live_row = jnp.broadcast_to(live[0][:, None], (shards, slots))
    nothing = jnp.zeros((shards, slots), BF)
    facts = jnp.concatenate(
        [v.astype(BF) for v in (req_hi, req_lo, lab_hi, lab_mid, lab_lo, live_row)]
        + [nothing, nothing],
        axis=1,
    ).reshape(shards, 2, uf)
    first = jnp.concatenate(
        [jnp.broadcast_to(user_feats, (shards, each, uf)), facts], axis=1
    )
    arrived = exchange(first)
    ids_rows = jnp.transpose(ids[0], (1, 0, 2)).reshape(ids.shape[2], shards * slots)
    items, counts = pool(ids_rows, table)
    feats = arrived[:, :each, :].reshape(reqs, uf)
    meta = jnp.transpose(
        arrived[:, each:, :].reshape(shards, 8, slots), (1, 0, 2)
    ).reshape(8, shards * slots)
    hid, slope, users = tower(feats, tower_in, tower_out, True)
    feats_all = [feats] + from_chips(feats)
    factor = 1.0 / math.sqrt(groups * shards * shards * slots)
    score, sent, gt = rank(
        factor, slots, shards, users, items, counts, meta, inter_weight, out_weight[:, None]
    )
    back = exchange(sent)
    towers = [(hid, slope)] + [tower(f, tower_in, tower_out, False) for f in feats_all[1:]]
    grad_table = group_sum(gt)
    summed = jnp.sum(back.astype(F32), axis=0)
    own = summed[:each].astype(BF)
    inter_part = group_sum(summed[each:].astype(BF))
    s_hi = to_bf(score.reshape(shards, slots))
    s_rest = score.reshape(shards, slots) - s_hi
    s_mid = to_bf(s_rest)
    s_lo = s_rest - s_mid
    score_row = jnp.concatenate(
        [s_hi.astype(BF), s_mid.astype(BF), s_lo.astype(BF)]
        + [jnp.zeros((shards, width - 3 * slots), BF)],
        axis=1,
    )[:, None, :]
    third = exchange(
        jnp.concatenate([jnp.broadcast_to(own, (shards, each, width)), score_row], axis=1)
    )
    d_own = third[:, :each, :].reshape(reqs, width)
    s_back = third[:, each, : 3 * slots].astype(F32)
    scores = (s_back[:, :slots] + s_back[:, slots : 2 * slots]) + s_back[:, 2 * slots :]
    d_all = [d_own] + from_chips(d_own)
    inter_all = exchange(jnp.broadcast_to(inter_part[:each].astype(BF), (shards, each, width)))
    half = shards // 2
    inter_flat = inter_all.astype(F32)
    grad_inter = jnp.concatenate(
        [inter_flat[:half].reshape(width, width), inter_flat[half:].reshape(width, width)], axis=1
    )
    grad_out = inter_part[each:].reshape(-1)
    g_out, g_in = dense(
        d_all,
        [f.T for f in feats_all],
        [t[0] for t in towers],
        [t[1] for t in towers],
        tower_out,
    )
    grad_tower_out = g_out.astype(F32) + swap(g_out).astype(F32)
    grad_tower_in = g_in.astype(F32) + swap(g_in).astype(F32)
    return (scores[None], grad_tower_in, grad_tower_out, grad_inter, grad_out, grad_table)


def solution(mesh):
    placed = (
        P(("grp", "tbl"), None),
        P(),
        P(),
        P("tbl", None),
        P(),
        P(),
        P(("grp", "tbl"), None, None, None),
        P(("grp", "tbl"), None),
        P(("grp", "tbl"), None, None),
        P(("grp", "tbl"), None, None),
    )
    return jax.shard_map(
        body,
        mesh=mesh,
        in_specs=placed,
        out_specs=(P(("grp", "tbl"), None, None), P(), P(), P(), P(), P("tbl", None)),
        check_vma=False,
    )
```

```python
import math

import jax
import jax.numpy as jnp
from jax import lax
from jax.experimental import pallas as pl
from jax.experimental.pallas import tpu as pltpu
from jax.sharding import PartitionSpec as P


BF = jnp.bfloat16
F32 = jnp.float32


def mm(a, b):
    return jnp.dot(a, b, preferred_element_type=F32)


def mm_nt(a, b):
    return lax.dot_general(a, b, (((1,), (1,)), ((), ())), preferred_element_type=F32)


def slope_of(value, sig):
    return sig * (1.0 + value * (1.0 - sig))


def pool_kernel(ids_ref, table_ref, items_ref, counts_ref):
    rows, cands = counts_ref.shape
    row = lax.broadcasted_iota(jnp.int32, (rows, cands), 0)
    total = jnp.zeros((rows, cands), F32)
    for b in range(ids_ref.shape[0]):
        total = total + jnp.where(row == ids_ref[b : b + 1, :], 1.0, 0.0)
    counts = total.astype(BF)
    counts_ref[...] = counts
    items_ref[...] = mm(table_ref[...].astype(F32).T.astype(BF), counts).astype(BF)


def pool(ids, table):
    cands = ids.shape[1]
    rows, width = table.shape
    return pl.pallas_call(
        pool_kernel,
        out_shape=(
            jax.ShapeDtypeStruct((width, cands), BF),
            jax.ShapeDtypeStruct((rows, cands), BF),
        ),
        compiler_params=pltpu.CompilerParams(vmem_limit_bytes=8 << 20),
        cost_estimate=pl.CostEstimate(
            flops=2 * cands * rows * width, bytes_accessed=2 << 20, transcendentals=0
        ),
        name="pool",
    )(ids, table)


def sigmoid(value):
    return 0.5 * jnp.tanh(0.5 * value) + 0.5


def hbm(array):
    return pltpu.with_memory_space_constraint(array, pltpu.HBM)


def flat(ref):
    value = ref[...]
    if len(value.shape) == 3:
        return value.reshape(value.shape[0] * value.shape[1], value.shape[2])
    half = value.shape[1] // 2
    return jnp.concatenate([value[:, :half], value[:, half:]], axis=0)


def feats_spec(array, each, uf):
    if len(array.shape) == 3:
        return pl.BlockSpec((array.shape[0], each, uf), lambda i: (0, 0, 0))
    return pl.BlockSpec((array.shape[0] // 2, 2 * uf), lambda i: (0, 0))


def users_kernel(feats_ref, win_ref, wout_ref, users_ref, acc):
    step = pl.program_id(0)
    half = mm_nt(win_ref[...], flat(feats_ref))
    part = mm(wout_ref[...], (half * jnp.tanh(half) + half).astype(BF))

    @pl.when(step == 0)
    def _():
        acc[...] = part

    @pl.when(step > 0)
    def _():
        acc[...] += part

    @pl.when(step == pl.num_programs(0) - 1)
    def _():
        users_ref[...] = acc[...].astype(BF)


def user_vectors(feats, win_t, wout_t, each):
    width, wide = wout_t.shape
    uf = win_t.shape[1]
    reqs = feats.shape[0] * each
    block = 512
    return pl.pallas_call(
        users_kernel,
        grid=(wide // block,),
        in_specs=[
            feats_spec(feats, each, uf),
            pl.BlockSpec((block, uf), lambda i: (i, 0)),
            pl.BlockSpec((width, block), lambda i: (0, i)),
        ],
        out_specs=pl.BlockSpec((width, reqs), lambda i: (0, 0)),
        out_shape=jax.ShapeDtypeStruct((width, reqs), BF),
        scratch_shapes=[pltpu.VMEM((width, reqs), F32)],
        compiler_params=pltpu.CompilerParams(vmem_limit_bytes=12 << 20),
        cost_estimate=pl.CostEstimate(
            flops=2 * reqs * wide * (uf + width),
            bytes_accessed=4 << 20,
            transcendentals=reqs * wide,
        ),
        name="users",
    )(feats, hbm(win_t), hbm(wout_t))


def hidden_of(feats, half_win):
    half = mm_nt(half_win, feats)
    turn = jnp.tanh(half)
    hid = half * turn + half
    rest = 0.5 - 0.5 * turn
    return hid.astype(BF), (1.0 - rest) + hid * rest


def rank_kernel(
    factor, slots, users_ref, items_ref, counts_ref, came_ref, iw_ref, w_ref,
    sent_ref, share_ref, acc_u, acc_g, acc_t, acc_o, acc_s,
):
    cands = items_ref.shape[1]
    reqs = users_ref.shape[1]
    width, _ = iw_ref.shape
    step_c = 256
    iw = iw_ref[...]
    iw_t = iw.astype(F32).T.astype(BF)
    weight = w_ref[...]
    users = users_ref[...]
    shards, _, uf = came_ref.shape
    each = reqs // shards
    near = step_c // slots
    came = came_ref[:, each : 2 * each, :].astype(F32)
    line = lax.broadcasted_iota(jnp.int32, came.shape, 1)
    facts = [jnp.sum(jnp.where(line == n, came, 0.0), axis=1) for n in range(2)]
    src = lax.broadcasted_iota(jnp.int32, (uf, step_c), 0)
    dst = lax.broadcasted_iota(jnp.int32, (uf, step_c), 1) % slots
    spread = [jnp.where(src == dst + n * slots, 1.0, 0.0).astype(BF) for n in range(4)]
    src = lax.broadcasted_iota(jnp.int32, (step_c, width), 0) % slots
    dst = lax.broadcasted_iota(jnp.int32, (step_c, width), 1)
    gather = [jnp.where(src + n * slots == dst, 1.0, 0.0).astype(BF) for n in range(3)]
    mine = (
        lax.broadcasted_iota(jnp.int32, (near, step_c), 0)
        == lax.broadcasted_iota(jnp.int32, (near, step_c), 1) // slots
    )
    slot = lax.broadcasted_iota(jnp.int32, (1, step_c), 1) % slots
    for k in range(cands // step_c):
        cut = slice(k * step_c, (k + 1) * step_c)
        meta = []
        for n in range(6):
            part = facts[n // 4][k * near : (k + 1) * near, :].astype(BF)
            wide_part = jnp.where(mine, mm(part, spread[n % 4]), 0.0)
            meta.append(jnp.sum(wide_part, axis=0, keepdims=True))
        request = (meta[0] * 16.0 + meta[1]).astype(jnp.int32)
        target = meta[2] + meta[3] + meta[4]
        live = meta[5]
        row = lax.broadcasted_iota(jnp.int32, (reqs, step_c), 0)
        pick = jnp.where(row == request, 1.0, 0.0).astype(BF)
        chosen = mm(users, pick)
        item = items_ref[:, cut].astype(F32)
        cross = (item * chosen).astype(BF)
        inner = mm(iw_t, cross)
        sig = sigmoid(inner)
        act = inner * sig
        score = jnp.sum(act * weight, axis=0, keepdims=True)
        s_hi = score.astype(BF).astype(F32)
        s_mid = (score - s_hi).astype(BF).astype(F32)
        row_out = jnp.zeros((near, width), F32)
        for n, v in enumerate((s_hi, s_mid, (score - s_hi) - s_mid)):
            row_out = row_out + mm(jnp.where(mine, v, 0.0).astype(BF), gather[n])
        acc_s[k * near : (k + 1) * near, :] = row_out
        grad = jnp.where(slot.astype(F32) < live, sigmoid(score) - target, 0.0) * factor
        dz = (grad * weight * slope_of(inner, sig)).astype(BF)
        dcross = mm(iw, dz)
        d_item = (dcross * chosen).astype(BF)
        d_user = (dcross * item).astype(BF)
        terms = mm_nt(pick, d_user)
        g_in = mm_nt(cross, dz)
        g_t = mm_nt(counts_ref[:, cut], d_item)
        g_o = mm_nt(jnp.broadcast_to(grad, (8, step_c)), act)
        if k == 0:
            acc_u[...] = terms
            acc_g[...] = g_in
            acc_t[...] = g_t
            acc_o[...] = g_o
        else:
            acc_u[...] += terms
            acc_g[...] += g_in
            acc_t[...] += g_t
            acc_o[...] += g_o
    sent_ref[:, 0:each, :] = acc_u[...].astype(BF).reshape(shards, each, width)
    half = shards // 2
    sent_ref[0:half, each : 2 * each, :] = acc_g[:, 0:width].astype(BF).reshape(half, each, width)
    sent_ref[half:, each : 2 * each, :] = acc_g[:, width:].astype(BF).reshape(half, each, width)
    line = lax.broadcasted_iota(jnp.int32, (shards, 4, width), 1)
    tail = jnp.where(
        line == 0,
        acc_o[0:1, 0:width][None],
        jnp.where(
            line == 1,
            acc_o[0:1, width:][None],
            jnp.where(line == 2, acc_s[...][:, None, :], 0.0),
        ),
    )
    sent_ref[:, 2 * each : 2 * each + 4, :] = tail.astype(BF)
    feats = came_ref[:, 0:each, :].reshape(reqs, uf)
    top = reqs // 2
    share_ref[0:top, 0:uf] = feats[0:top]
    share_ref[0:top, uf:] = feats[top:]
    share_ref[top:, :] = acc_t[...].astype(BF)


def rank(factor, slots, users, items, counts, came, iw, weight):
    width, cands = items.shape
    reqs = users.shape[1]
    hi_units = iw.shape[1]
    rows = counts.shape[0]
    shards = came.shape[0]
    each = reqs // shards
    return pl.pallas_call(
        lambda *refs: rank_kernel(factor, slots, *refs),
        out_shape=(
            jax.ShapeDtypeStruct((shards, 2 * each + 4, width), BF),
            jax.ShapeDtypeStruct((reqs // 2 + rows, width), BF),
        ),
        scratch_shapes=[
            pltpu.VMEM((reqs, width), F32),
            pltpu.VMEM((width, hi_units), F32),
            pltpu.VMEM((rows, width), F32),
            pltpu.VMEM((8, hi_units), F32),
            pltpu.VMEM((shards, width), F32),
        ],
        compiler_params=pltpu.CompilerParams(vmem_limit_bytes=16 << 20),
        cost_estimate=pl.CostEstimate(
            flops=2 * cands * width * (reqs * 2 + hi_units * 3 + rows),
            bytes_accessed=4 << 20,
            transcendentals=cands * hi_units,
        ),
        name="rank",
    )(users, items, counts, came, iw, weight)


def fold_kernel(back_ref, own_ref, part_ref):
    each, _ = own_ref.shape
    total = back_ref[0, 0 : 2 * each + 4, :].astype(F32)
    for n in range(1, back_ref.shape[0]):
        total = total + back_ref[n, 0 : 2 * each + 4, :].astype(F32)
    own_ref[...] = total[0:each].astype(BF)
    part_ref[...] = total[each:].astype(BF)


def fold(back, each):
    width = back.shape[2]
    return pl.pallas_call(
        fold_kernel,
        out_shape=(
            jax.ShapeDtypeStruct((each, width), BF),
            jax.ShapeDtypeStruct((each + 4, width), BF),
        ),
        compiler_params=pltpu.CompilerParams(vmem_limit_bytes=6 << 20),
        name="fold",
    )(back)


def own_kernel(d_ref, feats_ref, win_ref, wout_ref, gout_ref, gin_ref):
    feats = flat(feats_ref)
    d = flat(d_ref)
    hid, slope = hidden_of(feats, win_ref[...])
    gout_ref[...] = mm(hid, d)
    d_pre = (mm_nt(wout_ref[...], d) * slope).astype(BF)
    gin_ref[...] = mm(d_pre, feats).T


def dense_own(d, feats, win_t, tower_out, each):
    wide, width = tower_out.shape
    uf = win_t.shape[1]
    reqs = each * feats.shape[0]
    block = 512
    return pl.pallas_call(
        own_kernel,
        grid=(wide // block,),
        in_specs=[
            feats_spec(d, each, width),
            feats_spec(feats, each, uf),
            pl.BlockSpec((block, uf), lambda i: (i, 0)),
            pl.BlockSpec((block, width), lambda i: (i, 0)),
        ],
        out_specs=(
            pl.BlockSpec((block, width), lambda i: (i, 0)),
            pl.BlockSpec((uf, block), lambda i: (0, i)),
        ),
        out_shape=(pltpu.HBM((wide, width), F32), pltpu.HBM((uf, wide), F32)),
        compiler_params=pltpu.CompilerParams(vmem_limit_bytes=14 << 20),
        cost_estimate=pl.CostEstimate(
            flops=2 * reqs * wide * (2 * width + 2 * uf),
            bytes_accessed=10 << 20,
            transcendentals=reqs * wide,
        ),
        name="dense_own",
    )(d, feats, hbm(win_t), hbm(tower_out))


def far_kernel(count, *refs):
    d, feats = refs[0:count], refs[count : 2 * count]
    win_ref, wout_ref, old_out, old_in, gout_ref, gin_ref = refs[2 * count :]
    wout = wout_ref[...]
    win = win_ref[...]
    out, back = old_out[...], None
    for k in range(count):
        d_k = d[k][...]
        feats_k = flat(feats[k])
        hid, slope = hidden_of(feats_k, win)
        out = out + mm(hid, d_k)
        d_pre = (mm_nt(wout, d_k) * slope).astype(BF)
        turn = mm(d_pre, feats_k)
        back = turn if back is None else back + turn
    gout_ref[...] = out.astype(BF)
    gin_ref[...] = (back.T + old_in[...]).astype(BF)


def dense_far(d, feats, win_t, tower_out, before, first, units):
    _, width = tower_out.shape
    reqs = d[0].shape[0]
    uf = win_t.shape[1]
    count = len(d)
    block = 512
    base = first // block
    return pl.pallas_call(
        lambda *refs: far_kernel(count, *refs),
        grid=(units // block,),
        in_specs=[pl.BlockSpec((reqs, width), lambda i: (0, 0))] * count
        + [pl.BlockSpec((reqs // 2, 2 * uf), lambda i: (0, 0))] * count
        + [
            pl.BlockSpec((block, uf), lambda i: (base + i, 0)),
            pl.BlockSpec((block, width), lambda i: (base + i, 0)),
            pl.BlockSpec((block, width), lambda i: (base + i, 0)),
            pl.BlockSpec((uf, block), lambda i: (0, base + i)),
        ],
        out_specs=(
            pl.BlockSpec((block, width), lambda i: (i, 0)),
            pl.BlockSpec((uf, block), lambda i: (0, i)),
        ),
        out_shape=(
            jax.ShapeDtypeStruct((units, width), BF),
            jax.ShapeDtypeStruct((uf, units), BF),
        ),
        compiler_params=pltpu.CompilerParams(vmem_limit_bytes=20 << 20),
        cost_estimate=pl.CostEstimate(
            flops=2 * count * reqs * units * (2 * width + 2 * uf),
            bytes_accessed=10 << 20,
            transcendentals=count * reqs * units,
        ),
        name="dense_far",
    )(*[hbm(x) for x in (*d, *feats, win_t, tower_out, *before)])


def finish_kernel(*refs):
    out_a, out_b, in_a, in_b = refs[0:4]
    gout_ref, gin_ref = refs[-2:]
    gout_ref[...] = out_a[...].astype(F32) + out_b[...].astype(F32)
    gin_ref[...] = in_a[...].astype(F32) + in_b[...].astype(F32)


def finish(outs, ins, before, first, wide):
    units, width = outs[0].shape
    uf = ins[0].shape[0]
    block = 512
    base = first // block
    spec_o = pl.BlockSpec((block, width), lambda i: (i, 0))
    spec_i = pl.BlockSpec((uf, block), lambda i: (0, i))
    extra = [] if before is None else [pl.BlockSpec(memory_space=pl.ANY)] * 2
    return pl.pallas_call(
        finish_kernel,
        grid=(units // block,),
        in_specs=[spec_o, spec_o, spec_i, spec_i] + extra,
        out_specs=(
            pl.BlockSpec((block, width), lambda i: (base + i, 0)),
            pl.BlockSpec((uf, block), lambda i: (0, base + i)),
        ),
        out_shape=(pltpu.HBM((wide, width), F32), pltpu.HBM((uf, wide), F32)),
        input_output_aliases={} if before is None else {4: 0, 5: 1},
        compiler_params=pltpu.CompilerParams(vmem_limit_bytes=8 << 20),
        name="finish",
    )(*outs, *ins, *(before or ()))


def pack_kernel(feats_ref, req_ref, lab_ref, live_ref, out_ref):
    shards, slots = req_ref.shape
    each, lanes = feats_ref.shape
    req = req_ref[...].astype(F32)
    high = jnp.floor(req * (1.0 / 16.0))
    lab = lab_ref[...]
    lab_hi = lab.astype(BF).astype(F32)
    lab_mid = (lab - lab_hi).astype(BF).astype(F32)
    eye = lax.broadcasted_iota(jnp.int32, (shards, shards), 0) == lax.broadcasted_iota(
        jnp.int32, (shards, shards), 1
    )
    live = jnp.sum(
        jnp.where(eye, live_ref[...].astype(F32), 0.0), axis=1, keepdims=True
    )
    rows = []
    for group in (
        (high, req - high * 16.0, lab_hi, lab_mid),
        (lab - lab_hi - lab_mid, jnp.broadcast_to(live, (shards, slots))),
    ):
        total = jnp.zeros((shards, lanes), F32)
        for k, v in enumerate(group):
            src = lax.broadcasted_iota(jnp.int32, (slots, lanes), 0) + k * slots
            dst = lax.broadcasted_iota(jnp.int32, (slots, lanes), 1)
            total = total + mm(v.astype(BF), jnp.where(src == dst, 1.0, 0.0).astype(BF))
        rows.append(total)
    line = lax.broadcasted_iota(jnp.int32, (shards, each, lanes), 1)
    facts = jnp.where(
        line == 0, rows[0][:, None, :], jnp.where(line == 1, rows[1][:, None, :], 0.0)
    )
    out_ref[:, 0:each, :] = jnp.broadcast_to(feats_ref[...][None], (shards, each, lanes))
    out_ref[:, each : 2 * each, :] = facts.astype(BF)


def pack(feats, req, lab, live):
    each, lanes = feats.shape
    shards = req.shape[0]
    return pl.pallas_call(
        pack_kernel,
        out_shape=jax.ShapeDtypeStruct((shards, 2 * each, lanes), BF),
        compiler_params=pltpu.CompilerParams(vmem_limit_bytes=16 << 20),
        name="pack",
    )(*[hbm(x) for x in (feats, req, lab, live)])


def body(
    user_feats, tower_in, tower_out, table, inter_weight, out_weight, ids, live, req_of, labels
):
    groups = lax.axis_size("grp")
    shards = lax.axis_size("tbl")
    slots = ids.shape[3]
    width = table.shape[1]
    each = user_feats.shape[0]
    reqs = each * shards
    chips = groups // 2

    def ring(turn, other):
        return [
            (y * 2 + c, ((y + turn) % chips) * 2 + (c + other) % 2)
            for y in range(chips)
            for c in range(2)
        ]

    def from_chips(x):
        return [lax.ppermute(x, "grp", ring(turn, 0)) for turn in (1, chips - 1, 2)]

    def swap(x):
        return lax.ppermute(x, "grp", ring(0, 1))

    def group_sum(x):
        pair = (x.astype(F32) + swap(x).astype(F32)).astype(BF)
        a, b, c = from_chips(pair)
        return (pair.astype(F32) + c.astype(F32)) + (a.astype(F32) + b.astype(F32))

    def exchange(x):
        return lax.all_to_all(x, "tbl", split_axis=0, concat_axis=0, tiled=True)

    arrived = exchange(pack(user_feats, req_of[0], labels[0], live))
    ids_rows = jnp.transpose(ids[0], (1, 0, 2)).reshape(ids.shape[2], shards * slots)
    items, counts = pool(ids_rows, table)
    win_t = tower_in.T * jnp.asarray(0.5, BF)
    wout_t = tower_out.T
    users = user_vectors(arrived, win_t, wout_t, each)
    factor = 1.0 / math.sqrt(groups * shards * shards * slots)
    sent, share = rank(
        factor, slots, users, items, counts, arrived, inter_weight, out_weight[:, None]
    )
    back = exchange(sent)
    far = from_chips(share)
    own, part = fold(back, each)
    third = exchange(jnp.broadcast_to(own, (shards, each, width)))
    total = group_sum(part)
    grad_out = total[each : each + 2].reshape(-1)
    s_back = back[:, 2 * each + 2, : 3 * slots].astype(F32)
    scores = (s_back[:, :slots] + s_back[:, slots : 2 * slots]) + s_back[:, 2 * slots :]
    top = reqs // 2
    a, b, c = (f[top:].astype(F32) for f in far)
    column = ((share[top:].astype(F32) + c) + (a + b)).astype(BF)
    grad_table = column.astype(F32) + swap(column).astype(F32)
    d_far = from_chips(third.reshape(reqs, width))
    inter_all = exchange(
        jnp.broadcast_to(total[:each].astype(BF), (shards, each, width))
    )
    before = dense_own(third, arrived, win_t, tower_out, each)
    half = shards // 2
    inter_flat = inter_all.astype(F32)
    grad_inter = jnp.concatenate(
        [inter_flat[:half].reshape(width, width), inter_flat[half:].reshape(width, width)],
        axis=1,
    )
    units = tower_out.shape[0] // 2
    sums = None
    pieces = []
    for k in range(2):
        g_out, g_in = dense_far(d_far, far, win_t, tower_out, before, k * units, units)
        pieces.append(((g_out, swap(g_out)), (g_in, swap(g_in))))
    for k in range(2):
        sums = finish(*pieces[k], sums, k * units, 2 * units)
    return (scores[None], sums[1], sums[0], grad_inter, grad_out, grad_table)


def solution(mesh):
    placed = (
        P(("grp", "tbl"), None),
        P(),
        P(),
        P("tbl", None),
        P(),
        P(),
        P(("grp", "tbl"), None, None, None),
        P(("grp", "tbl"), None),
        P(("grp", "tbl"), None, None),
        P(("grp", "tbl"), None, None),
    )
    return jax.shard_map(
        body,
        mesh=mesh,
        in_specs=placed,
        out_specs=(P(("grp", "tbl"), None, None), P(), P(), P(), P(), P("tbl", None)),
        check_vma=False,
    )
```

```python
import math

import jax
import jax.numpy as jnp
from jax import lax
from jax.experimental import pallas as pl
from jax.experimental.pallas import tpu as pltpu
from jax.sharding import PartitionSpec as P


BF = jnp.bfloat16
F32 = jnp.float32


def mm(a, b):
    return jnp.dot(a, b, preferred_element_type=F32)


def mm_nt(a, b):
    return lax.dot_general(a, b, (((1,), (1,)), ((), ())), preferred_element_type=F32)


def pool_kernel(ids_ref, table_ref, items_ref, counts_ref):
    rows, cands = counts_ref.shape
    row = lax.broadcasted_iota(jnp.int32, (rows, cands), 0)
    total = jnp.zeros((rows, cands), F32)
    for b in range(ids_ref.shape[0]):
        total = total + jnp.where(row == ids_ref[b : b + 1, :], 1.0, 0.0)
    counts = total.astype(BF)
    counts_ref[...] = counts
    items_ref[...] = mm(table_ref[...].astype(F32).T.astype(BF), counts).astype(BF)


def pool(ids, table):
    cands = ids.shape[1]
    rows, width = table.shape
    return pl.pallas_call(
        pool_kernel,
        out_shape=(
            jax.ShapeDtypeStruct((width, cands), BF),
            jax.ShapeDtypeStruct((rows, cands), BF),
        ),
        compiler_params=pltpu.CompilerParams(vmem_limit_bytes=8 << 20),
        cost_estimate=pl.CostEstimate(
            flops=2 * cands * rows * width, bytes_accessed=2 << 20, transcendentals=0
        ),
        name="pool",
    )(ids, table)


def sigmoid(value):
    return 0.5 * jnp.tanh(0.5 * value) + 0.5


def hbm(array):
    return pltpu.with_memory_space_constraint(array, pltpu.HBM)


def flat(ref):
    value = ref[...]
    if len(value.shape) == 3:
        return value.reshape(value.shape[0] * value.shape[1], value.shape[2])
    half = value.shape[1] // 2
    return jnp.concatenate([value[:, :half], value[:, half:]], axis=0)


def feats_spec(array, each, uf):
    if len(array.shape) == 3:
        return pl.BlockSpec((array.shape[0], each, uf), lambda i: (0, 0, 0))
    return pl.BlockSpec((array.shape[0] // 2, 2 * uf), lambda i: (0, 0))


def users_kernel(feats_ref, win_ref, wout_ref, users_ref, acc):
    step = pl.program_id(0)
    half = mm(flat(feats_ref) * jnp.asarray(0.5, BF), win_ref[...])
    part = mm((half * jnp.tanh(half) + half).astype(BF), wout_ref[...])

    @pl.when(step == 0)
    def _():
        acc[...] = part

    @pl.when(step > 0)
    def _():
        acc[...] += part

    @pl.when(step == pl.num_programs(0) - 1)
    def _():
        users_ref[...] = acc[...].T.astype(BF)


def user_vectors(feats, tower_in, tower_out, each):
    wide, width = tower_out.shape
    uf = tower_in.shape[0]
    reqs = feats.shape[0] * each
    block = 2048
    return pl.pallas_call(
        users_kernel,
        grid=(wide // block,),
        in_specs=[
            feats_spec(feats, each, uf),
            pl.BlockSpec((uf, block), lambda i: (0, i)),
            pl.BlockSpec((block, width), lambda i: (i, 0)),
        ],
        out_specs=pl.BlockSpec((width, reqs), lambda i: (0, 0)),
        out_shape=jax.ShapeDtypeStruct((width, reqs), BF),
        scratch_shapes=[pltpu.VMEM((reqs, width), F32)],
        compiler_params=pltpu.CompilerParams(vmem_limit_bytes=16 << 20),
        cost_estimate=pl.CostEstimate(
            flops=2 * reqs * wide * (uf + width),
            bytes_accessed=4 << 20,
            transcendentals=reqs * wide,
        ),
        name="users",
    )(feats, hbm(tower_in), hbm(tower_out))


def hidden_of(feats, win):
    half = mm_nt(win, feats * jnp.asarray(0.5, BF))
    turn = jnp.tanh(half)
    hid = half * turn + half
    rest = 0.5 - 0.5 * turn
    return hid.astype(BF), (1.0 - rest) + hid * rest


def rank_kernel(
    factor, slots, users_ref, items_ref, counts_ref, came_ref, iw_ref, w_ref,
    sent_ref, share_ref, acc_u, acc_g, acc_t, acc_o, acc_s,
):
    cands = items_ref.shape[1]
    reqs = users_ref.shape[1]
    width, _ = iw_ref.shape
    step_c = 256
    iw = iw_ref[...]
    iw_t = (iw.astype(F32) * 0.5).T.astype(BF)
    weight = w_ref[...]
    users = users_ref[...]
    shards, _, uf = came_ref.shape
    each = reqs // shards
    near = step_c // slots
    came = came_ref[:, each : 2 * each, :].astype(F32)
    line = lax.broadcasted_iota(jnp.int32, came.shape, 1)
    facts = [jnp.sum(jnp.where(line == n, came, 0.0), axis=1) for n in range(2)]
    src = lax.broadcasted_iota(jnp.int32, (uf, step_c), 0)
    dst = lax.broadcasted_iota(jnp.int32, (uf, step_c), 1) % slots
    spread = [jnp.where(src == dst + n * slots, 1.0, 0.0).astype(BF) for n in range(4)]
    src = lax.broadcasted_iota(jnp.int32, (step_c, width), 0) % slots
    dst = lax.broadcasted_iota(jnp.int32, (step_c, width), 1)
    gather = [jnp.where(src + n * slots == dst, 1.0, 0.0).astype(BF) for n in range(3)]
    mine = (
        lax.broadcasted_iota(jnp.int32, (near, step_c), 0)
        == lax.broadcasted_iota(jnp.int32, (near, step_c), 1) // slots
    )
    slot = lax.broadcasted_iota(jnp.int32, (1, step_c), 1) % slots
    for k in range(cands // step_c):
        cut = slice(k * step_c, (k + 1) * step_c)
        meta = []
        for n in range(6):
            part = facts[n // 4][k * near : (k + 1) * near, :].astype(BF)
            wide_part = jnp.where(mine, mm(part, spread[n % 4]), 0.0)
            meta.append(jnp.sum(wide_part, axis=0, keepdims=True))
        request = (meta[0] * 16.0 + meta[1]).astype(jnp.int32)
        target = meta[2] + meta[3] + meta[4]
        live = meta[5]
        row = lax.broadcasted_iota(jnp.int32, (reqs, step_c), 0)
        pick = jnp.where(row == request, 1.0, 0.0).astype(BF)
        chosen = mm(users, pick)
        item = items_ref[:, cut].astype(F32)
        cross = (item * chosen).astype(BF)
        half = mm(iw_t, cross)
        turn = jnp.tanh(half)
        act = half * turn + half
        rest = 0.5 - 0.5 * turn
        score = jnp.sum(act * weight, axis=0, keepdims=True)
        s_hi = score.astype(BF).astype(F32)
        s_mid = (score - s_hi).astype(BF).astype(F32)
        row_out = jnp.zeros((near, width), F32)
        for n, v in enumerate((s_hi, s_mid, (score - s_hi) - s_mid)):
            row_out = row_out + mm(jnp.where(mine, v, 0.0).astype(BF), gather[n])
        acc_s[k * near : (k + 1) * near, :] = row_out
        grad = jnp.where(slot.astype(F32) < live, sigmoid(score) - target, 0.0) * factor
        dz = (grad * weight * ((1.0 - rest) + act * rest)).astype(BF)
        dcross = mm(iw, dz)
        d_item = (dcross * chosen).astype(BF)
        d_user = (dcross * item).astype(BF)
        terms = mm_nt(pick, d_user)
        g_in = mm_nt(cross, dz)
        g_t = mm_nt(counts_ref[:, cut], d_item)
        g_o = mm_nt(jnp.broadcast_to(grad, (8, step_c)), act)
        if k == 0:
            acc_u[...] = terms
            acc_g[...] = g_in
            acc_t[...] = g_t
            acc_o[...] = g_o
        else:
            acc_u[...] += terms
            acc_g[...] += g_in
            acc_t[...] += g_t
            acc_o[...] += g_o
    sent_ref[:, 0:each, :] = acc_u[...].astype(BF).reshape(shards, each, width)
    half = shards // 2
    sent_ref[0:half, each : 2 * each, :] = acc_g[:, 0:width].astype(BF).reshape(half, each, width)
    sent_ref[half:, each : 2 * each, :] = acc_g[:, width:].astype(BF).reshape(half, each, width)
    line = lax.broadcasted_iota(jnp.int32, (shards, 4, width), 1)
    tail = jnp.where(
        line == 0,
        acc_o[0:1, 0:width][None],
        jnp.where(
            line == 1,
            acc_o[0:1, width:][None],
            jnp.where(line == 2, acc_s[...][:, None, :], 0.0),
        ),
    )
    sent_ref[:, 2 * each : 2 * each + 4, :] = tail.astype(BF)
    feats = came_ref[:, 0:each, :].reshape(reqs, uf)
    top = reqs // 2
    share_ref[0:top, 0:uf] = feats[0:top]
    share_ref[0:top, uf:] = feats[top:]
    share_ref[top:, :] = acc_t[...].astype(BF)


def rank(factor, slots, users, items, counts, came, iw, weight):
    width, cands = items.shape
    reqs = users.shape[1]
    hi_units = iw.shape[1]
    rows = counts.shape[0]
    shards = came.shape[0]
    each = reqs // shards
    return pl.pallas_call(
        lambda *refs: rank_kernel(factor, slots, *refs),
        out_shape=(
            jax.ShapeDtypeStruct((shards, 2 * each + 4, width), BF),
            jax.ShapeDtypeStruct((reqs // 2 + rows, width), BF),
        ),
        scratch_shapes=[
            pltpu.VMEM((reqs, width), F32),
            pltpu.VMEM((width, hi_units), F32),
            pltpu.VMEM((rows, width), F32),
            pltpu.VMEM((8, hi_units), F32),
            pltpu.VMEM((shards, width), F32),
        ],
        compiler_params=pltpu.CompilerParams(vmem_limit_bytes=16 << 20),
        cost_estimate=pl.CostEstimate(
            flops=2 * cands * width * (reqs * 2 + hi_units * 3 + rows),
            bytes_accessed=4 << 20,
            transcendentals=cands * hi_units,
        ),
        name="rank",
    )(users, items, counts, came, iw, weight)


def fold_kernel(back_ref, own_ref, part_ref):
    each, _ = own_ref.shape
    total = back_ref[0, 0 : 2 * each + 4, :].astype(F32)
    for n in range(1, back_ref.shape[0]):
        total = total + back_ref[n, 0 : 2 * each + 4, :].astype(F32)
    own_ref[...] = total[0:each].astype(BF)
    part_ref[...] = total[each:].astype(BF)


def fold(back, each):
    width = back.shape[2]
    return pl.pallas_call(
        fold_kernel,
        out_shape=(
            jax.ShapeDtypeStruct((each, width), BF),
            jax.ShapeDtypeStruct((each + 4, width), BF),
        ),
        compiler_params=pltpu.CompilerParams(vmem_limit_bytes=6 << 20),
        name="fold",
    )(back)


def own_kernel(d_ref, feats_ref, win_ref, wout_ref, gout_ref, gin_ref):
    feats = flat(feats_ref)
    d = flat(d_ref)
    hid, slope = hidden_of(feats, win_ref[...])
    gout_ref[...] = mm(hid, d)
    d_pre = (mm_nt(wout_ref[...], d) * slope).astype(BF)
    gin_ref[...] = mm(d_pre, feats).T


def dense_own(d, feats, win_t, tower_out, each):
    wide, width = tower_out.shape
    uf = win_t.shape[1]
    reqs = each * feats.shape[0]
    block = 1024
    return pl.pallas_call(
        own_kernel,
        grid=(wide // block,),
        in_specs=[
            feats_spec(d, each, width),
            feats_spec(feats, each, uf),
            pl.BlockSpec((block, uf), lambda i: (i, 0)),
            pl.BlockSpec((block, width), lambda i: (i, 0)),
        ],
        out_specs=(
            pl.BlockSpec((block, width), lambda i: (i, 0)),
            pl.BlockSpec((uf, block), lambda i: (0, i)),
        ),
        out_shape=(pltpu.HBM((wide, width), F32), pltpu.HBM((uf, wide), F32)),
        compiler_params=pltpu.CompilerParams(vmem_limit_bytes=28 << 20),
        cost_estimate=pl.CostEstimate(
            flops=2 * reqs * wide * (2 * width + 2 * uf),
            bytes_accessed=10 << 20,
            transcendentals=reqs * wide,
        ),
        name="dense_own",
    )(d, feats, hbm(win_t), hbm(tower_out))


def far_kernel(count, *refs):
    d, feats = refs[0:count], refs[count : 2 * count]
    win_ref, wout_ref, old_out, old_in, gout_ref, gin_ref = refs[2 * count :]
    wout = wout_ref[...]
    win = win_ref[...]
    d_all = jnp.concatenate([x[...] for x in d], axis=0)
    feats_all = jnp.concatenate([flat(x) for x in feats], axis=0)
    reqs = d[0].shape[0]
    hids, pres = [], []
    for k in range(count):
        hid, slope = hidden_of(feats_all[k * reqs : (k + 1) * reqs], win)
        hids.append(hid)
        pres.append((mm_nt(wout, d_all[k * reqs : (k + 1) * reqs]) * slope).astype(BF))
    out = old_out[...] + mm(jnp.concatenate(hids, axis=1), d_all)
    back = mm(jnp.concatenate(pres, axis=1), feats_all)
    gout_ref[...] = out.astype(BF)
    gin_ref[...] = (back.T + old_in[...]).astype(BF)


def dense_far(d, feats, win_t, tower_out, before, first, units):
    _, width = tower_out.shape
    reqs = d[0].shape[0]
    uf = win_t.shape[1]
    count = len(d)
    block = 512
    base = first // block
    return pl.pallas_call(
        lambda *refs: far_kernel(count, *refs),
        grid=(units // block,),
        in_specs=[pl.BlockSpec((reqs, width), lambda i: (0, 0))] * count
        + [pl.BlockSpec((reqs // 2, 2 * uf), lambda i: (0, 0))] * count
        + [
            pl.BlockSpec((block, uf), lambda i: (base + i, 0)),
            pl.BlockSpec((block, width), lambda i: (base + i, 0)),
            pl.BlockSpec((block, width), lambda i: (base + i, 0)),
            pl.BlockSpec((uf, block), lambda i: (0, base + i)),
        ],
        out_specs=(
            pl.BlockSpec((block, width), lambda i: (i, 0)),
            pl.BlockSpec((uf, block), lambda i: (0, i)),
        ),
        out_shape=(
            jax.ShapeDtypeStruct((units, width), BF),
            jax.ShapeDtypeStruct((uf, units), BF),
        ),
        compiler_params=pltpu.CompilerParams(vmem_limit_bytes=36 << 20),
        cost_estimate=pl.CostEstimate(
            flops=2 * count * reqs * units * (2 * width + 2 * uf),
            bytes_accessed=10 << 20,
            transcendentals=count * reqs * units,
        ),
        name="dense_far",
    )(*[hbm(x) for x in (*d, *feats, win_t, tower_out, *before)])


def finish_kernel(*refs):
    out_a, out_b, in_a, in_b = refs[0:4]
    gout_ref, gin_ref = refs[-2:]
    gout_ref[...] = out_a[...].astype(F32) + out_b[...].astype(F32)
    gin_ref[...] = in_a[...].astype(F32) + in_b[...].astype(F32)


def finish(outs, ins, before, first, wide):
    units, width = outs[0].shape
    uf = ins[0].shape[0]
    block = 512
    base = first // block
    spec_o = pl.BlockSpec((block, width), lambda i: (i, 0))
    spec_i = pl.BlockSpec((uf, block), lambda i: (0, i))
    extra = [] if before is None else [pl.BlockSpec(memory_space=pl.ANY)] * 2
    return pl.pallas_call(
        finish_kernel,
        grid=(units // block,),
        in_specs=[spec_o, spec_o, spec_i, spec_i] + extra,
        out_specs=(
            pl.BlockSpec((block, width), lambda i: (base + i, 0)),
            pl.BlockSpec((uf, block), lambda i: (0, base + i)),
        ),
        out_shape=(pltpu.HBM((wide, width), F32), pltpu.HBM((uf, wide), F32)),
        input_output_aliases={} if before is None else {4: 0, 5: 1},
        compiler_params=pltpu.CompilerParams(vmem_limit_bytes=8 << 20),
        name="finish",
    )(*outs, *ins, *(before or ()))


def pack_kernel(feats_ref, req_ref, lab_ref, live_ref, out_ref):
    shards, slots = req_ref.shape
    each, lanes = feats_ref.shape
    req = req_ref[...].astype(F32)
    high = jnp.floor(req * (1.0 / 16.0))
    lab = lab_ref[...]
    lab_hi = lab.astype(BF).astype(F32)
    lab_mid = (lab - lab_hi).astype(BF).astype(F32)
    eye = lax.broadcasted_iota(jnp.int32, (shards, shards), 0) == lax.broadcasted_iota(
        jnp.int32, (shards, shards), 1
    )
    live = jnp.sum(
        jnp.where(eye, live_ref[...].astype(F32), 0.0), axis=1, keepdims=True
    )
    rows = []
    for group in (
        (high, req - high * 16.0, lab_hi, lab_mid),
        (lab - lab_hi - lab_mid, jnp.broadcast_to(live, (shards, slots))),
    ):
        total = jnp.zeros((shards, lanes), F32)
        for k, v in enumerate(group):
            src = lax.broadcasted_iota(jnp.int32, (slots, lanes), 0) + k * slots
            dst = lax.broadcasted_iota(jnp.int32, (slots, lanes), 1)
            total = total + mm(v.astype(BF), jnp.where(src == dst, 1.0, 0.0).astype(BF))
        rows.append(total)
    line = lax.broadcasted_iota(jnp.int32, (shards, each, lanes), 1)
    facts = jnp.where(
        line == 0, rows[0][:, None, :], jnp.where(line == 1, rows[1][:, None, :], 0.0)
    )
    out_ref[:, 0:each, :] = jnp.broadcast_to(feats_ref[...][None], (shards, each, lanes))
    out_ref[:, each : 2 * each, :] = facts.astype(BF)


def pack(feats, req, lab, live):
    each, lanes = feats.shape
    shards = req.shape[0]
    return pl.pallas_call(
        pack_kernel,
        out_shape=jax.ShapeDtypeStruct((shards, 2 * each, lanes), BF),
        compiler_params=pltpu.CompilerParams(vmem_limit_bytes=16 << 20),
        name="pack",
    )(*[hbm(x) for x in (feats, req, lab, live)])


def body(
    user_feats, tower_in, tower_out, table, inter_weight, out_weight, ids, live, req_of, labels
):
    groups = lax.axis_size("grp")
    shards = lax.axis_size("tbl")
    slots = ids.shape[3]
    width = table.shape[1]
    each = user_feats.shape[0]
    reqs = each * shards
    chips = groups // 2

    def ring(turn, other):
        return [
            (y * 2 + c, ((y + turn) % chips) * 2 + (c + other) % 2)
            for y in range(chips)
            for c in range(2)
        ]

    def from_chips(x):
        return [lax.ppermute(x, "grp", ring(turn, 0)) for turn in (1, chips - 1, 2)]

    def swap(x):
        return lax.ppermute(x, "grp", ring(0, 1))

    def group_sum(x):
        pair = (x.astype(F32) + swap(x).astype(F32)).astype(BF)
        a, b, c = from_chips(pair)
        return (pair.astype(F32) + c.astype(F32)) + (a.astype(F32) + b.astype(F32))

    def exchange(x):
        return lax.all_to_all(x, "tbl", split_axis=0, concat_axis=0, tiled=True)

    arrived = exchange(pack(user_feats, req_of[0], labels[0], live))
    ids_rows = jnp.transpose(ids[0], (1, 0, 2)).reshape(ids.shape[2], shards * slots)
    items, counts = pool(ids_rows, table)
    win_t = tower_in.T
    users = user_vectors(arrived, tower_in, tower_out, each)
    factor = 1.0 / math.sqrt(groups * shards * shards * slots)
    sent, share = rank(
        factor, slots, users, items, counts, arrived, inter_weight, out_weight[:, None]
    )
    back = exchange(sent)
    far = from_chips(share)
    own, part = fold(back, each)
    third = exchange(jnp.broadcast_to(own, (shards, each, width)))
    total = group_sum(part)
    grad_out = total[each : each + 2].reshape(-1)
    s_back = back[:, 2 * each + 2, : 3 * slots].astype(F32)
    scores = (s_back[:, :slots] + s_back[:, slots : 2 * slots]) + s_back[:, 2 * slots :]
    top = reqs // 2
    a, b, c = (f[top:].astype(F32) for f in far)
    column = ((share[top:].astype(F32) + c) + (a + b)).astype(BF)
    grad_table = column.astype(F32) + swap(column).astype(F32)
    d_far = from_chips(third.reshape(reqs, width))
    inter_all = exchange(
        jnp.broadcast_to(total[:each].astype(BF), (shards, each, width))
    )
    before = dense_own(third, arrived, win_t, tower_out, each)
    half = shards // 2
    inter_flat = inter_all.astype(F32)
    grad_inter = jnp.concatenate(
        [inter_flat[:half].reshape(width, width), inter_flat[half:].reshape(width, width)],
        axis=1,
    )
    units = tower_out.shape[0] // 2
    sums = None
    pieces = []
    for k in range(2):
        g_out, g_in = dense_far(d_far, far, win_t, tower_out, before, k * units, units)
        pieces.append(((g_out, swap(g_out)), (g_in, swap(g_in))))
    for k in range(2):
        sums = finish(*pieces[k], sums, k * units, 2 * units)
    return (scores[None], sums[1], sums[0], grad_inter, grad_out, grad_table)


def solution(mesh):
    placed = (
        P(("grp", "tbl"), None),
        P(),
        P(),
        P("tbl", None),
        P(),
        P(),
        P(("grp", "tbl"), None, None, None),
        P(("grp", "tbl"), None),
        P(("grp", "tbl"), None, None),
        P(("grp", "tbl"), None, None),
    )
    return jax.shard_map(
        body,
        mesh=mesh,
        in_specs=placed,
        out_specs=(P(("grp", "tbl"), None, None), P(), P(), P(), P(), P("tbl", None)),
        check_vma=False,
    )
```

```python
import math

import jax
import jax.numpy as jnp
from jax import lax
from jax.experimental import pallas as pl
from jax.experimental.pallas import tpu as pltpu
from jax.sharding import PartitionSpec as P


BF = jnp.bfloat16
F32 = jnp.float32


def mm(a, b):
    return jnp.dot(a, b, preferred_element_type=F32)


def mm_nt(a, b):
    return lax.dot_general(a, b, (((1,), (1,)), ((), ())), preferred_element_type=F32)


def pool_kernel(ids_ref, table_ref, items_ref, counts_ref):
    rows, cands = counts_ref.shape
    row = lax.broadcasted_iota(jnp.int32, (rows, cands), 0)
    total = jnp.zeros((rows, cands), F32)
    for b in range(ids_ref.shape[0]):
        total = total + jnp.where(row == ids_ref[b : b + 1, :], 1.0, 0.0)
    counts = total.astype(BF)
    counts_ref[...] = counts
    items_ref[...] = mm(table_ref[...].astype(F32).T.astype(BF), counts).astype(BF)


def pool(ids, table):
    cands = ids.shape[1]
    rows, width = table.shape
    return pl.pallas_call(
        pool_kernel,
        out_shape=(
            jax.ShapeDtypeStruct((width, cands), BF),
            jax.ShapeDtypeStruct((rows, cands), BF),
        ),
        compiler_params=pltpu.CompilerParams(vmem_limit_bytes=8 << 20),
        cost_estimate=pl.CostEstimate(
            flops=2 * cands * rows * width, bytes_accessed=2 << 20, transcendentals=0
        ),
        name="pool",
    )(ids, table)


def sigmoid(value):
    return 0.5 * jnp.tanh(0.5 * value) + 0.5


def hbm(array):
    return pltpu.with_memory_space_constraint(array, pltpu.HBM)


def flat(ref):
    value = ref[...]
    if len(value.shape) == 3:
        return value.reshape(value.shape[0] * value.shape[1], value.shape[2])
    half = value.shape[1] // 2
    return jnp.concatenate([value[:, :half], value[:, half:]], axis=0)


def feats_spec(array, each, uf):
    if len(array.shape) == 3:
        return pl.BlockSpec((array.shape[0], each, uf), lambda i: (0, 0, 0))
    return pl.BlockSpec((array.shape[0] // 2, 2 * uf), lambda i: (0, 0))


def users_kernel(feats_ref, win_ref, wout_ref, users_ref, acc):
    step = pl.program_id(0)
    half = mm(flat(feats_ref) * jnp.asarray(0.5, BF), win_ref[...])
    part = mm((half * jnp.tanh(half) + half).astype(BF), wout_ref[...])

    @pl.when(step == 0)
    def _():
        acc[...] = part

    @pl.when(step > 0)
    def _():
        acc[...] += part

    @pl.when(step == pl.num_programs(0) - 1)
    def _():
        users_ref[...] = acc[...].T.astype(BF)


def user_vectors(feats, tower_in, tower_out, each):
    wide, width = tower_out.shape
    uf = tower_in.shape[0]
    reqs = feats.shape[0] * each
    block = 2048
    return pl.pallas_call(
        users_kernel,
        grid=(wide // block,),
        in_specs=[
            feats_spec(feats, each, uf),
            pl.BlockSpec((uf, block), lambda i: (0, i)),
            pl.BlockSpec((block, width), lambda i: (i, 0)),
        ],
        out_specs=pl.BlockSpec((width, reqs), lambda i: (0, 0)),
        out_shape=jax.ShapeDtypeStruct((width, reqs), BF),
        scratch_shapes=[pltpu.VMEM((reqs, width), F32)],
        compiler_params=pltpu.CompilerParams(vmem_limit_bytes=16 << 20),
        cost_estimate=pl.CostEstimate(
            flops=2 * reqs * wide * (uf + width),
            bytes_accessed=4 << 20,
            transcendentals=reqs * wide,
        ),
        name="users",
    )(feats, hbm(tower_in), hbm(tower_out))


def hidden_of(feats, win):
    half = mm_nt(win, feats * jnp.asarray(0.5, BF))
    turn = jnp.tanh(half)
    hid = half * turn + half
    rest = 0.5 - 0.5 * turn
    return hid.astype(BF), (1.0 - rest) + hid * rest


def rank_kernel(
    factor, slots, users_ref, items_ref, counts_ref, came_ref, iw_ref, w_ref,
    sent_ref, share_ref, acc_u, acc_g, acc_t, acc_o, acc_s,
):
    cands = items_ref.shape[1]
    reqs = users_ref.shape[1]
    width, _ = iw_ref.shape
    step_c = 256
    iw = iw_ref[...]
    iw_t = (iw.astype(F32) * 0.5).T.astype(BF)
    weight = w_ref[...]
    users = users_ref[...]
    shards, _, uf = came_ref.shape
    each = reqs // shards
    near = step_c // slots
    came = came_ref[:, each : 2 * each, :].astype(F32)
    line = lax.broadcasted_iota(jnp.int32, came.shape, 1)
    facts = [jnp.sum(jnp.where(line == n, came, 0.0), axis=1) for n in range(2)]
    src = lax.broadcasted_iota(jnp.int32, (uf, step_c), 0)
    dst = lax.broadcasted_iota(jnp.int32, (uf, step_c), 1) % slots
    spread = [jnp.where(src == dst + n * slots, 1.0, 0.0).astype(BF) for n in range(4)]
    src = lax.broadcasted_iota(jnp.int32, (step_c, width), 0) % slots
    dst = lax.broadcasted_iota(jnp.int32, (step_c, width), 1)
    gather = [jnp.where(src + n * slots == dst, 1.0, 0.0).astype(BF) for n in range(3)]
    mine = (
        lax.broadcasted_iota(jnp.int32, (near, step_c), 0)
        == lax.broadcasted_iota(jnp.int32, (near, step_c), 1) // slots
    )
    slot = lax.broadcasted_iota(jnp.int32, (1, step_c), 1) % slots
    for k in range(cands // step_c):
        cut = slice(k * step_c, (k + 1) * step_c)
        meta = []
        for n in range(6):
            part = facts[n // 4][k * near : (k + 1) * near, :].astype(BF)
            wide_part = jnp.where(mine, mm(part, spread[n % 4]), 0.0)
            meta.append(jnp.sum(wide_part, axis=0, keepdims=True))
        request = (meta[0] * 16.0 + meta[1]).astype(jnp.int32)
        target = meta[2] + meta[3] + meta[4]
        live = meta[5]
        row = lax.broadcasted_iota(jnp.int32, (reqs, step_c), 0)
        pick = jnp.where(row == request, 1.0, 0.0).astype(BF)
        chosen = mm(users, pick)
        item = items_ref[:, cut].astype(F32)
        cross = (item * chosen).astype(BF)
        half = mm(iw_t, cross)
        turn = jnp.tanh(half)
        act = half * turn + half
        rest = 0.5 - 0.5 * turn
        score = jnp.sum(act * weight, axis=0, keepdims=True)
        s_hi = score.astype(BF).astype(F32)
        s_mid = (score - s_hi).astype(BF).astype(F32)
        row_out = jnp.zeros((near, width), F32)
        for n, v in enumerate((s_hi, s_mid, (score - s_hi) - s_mid)):
            row_out = row_out + mm(jnp.where(mine, v, 0.0).astype(BF), gather[n])
        acc_s[k * near : (k + 1) * near, :] = row_out
        grad = jnp.where(slot.astype(F32) < live, sigmoid(score) - target, 0.0) * factor
        dz = (grad * weight * ((1.0 - rest) + act * rest)).astype(BF)
        dcross = mm(iw, dz)
        d_item = (dcross * chosen).astype(BF)
        d_user = (dcross * item).astype(BF)
        terms = mm_nt(pick, d_user)
        g_in = mm_nt(cross, dz)
        g_t = mm_nt(counts_ref[:, cut], d_item)
        g_o = mm_nt(jnp.broadcast_to(grad, (8, step_c)), act)
        if k == 0:
            acc_u[...] = terms
            acc_g[...] = g_in
            acc_t[...] = g_t
            acc_o[...] = g_o
        else:
            acc_u[...] += terms
            acc_g[...] += g_in
            acc_t[...] += g_t
            acc_o[...] += g_o
    sent_ref[:, 0:each, :] = acc_u[...].astype(BF).reshape(shards, each, width)
    half = shards // 2
    sent_ref[0:half, each : 2 * each, :] = acc_g[:, 0:width].astype(BF).reshape(half, each, width)
    sent_ref[half:, each : 2 * each, :] = acc_g[:, width:].astype(BF).reshape(half, each, width)
    line = lax.broadcasted_iota(jnp.int32, (shards, 4, width), 1)
    tail = jnp.where(
        line == 0,
        acc_o[0:1, 0:width][None],
        jnp.where(
            line == 1,
            acc_o[0:1, width:][None],
            jnp.where(line == 2, acc_s[...][:, None, :], 0.0),
        ),
    )
    sent_ref[:, 2 * each : 2 * each + 4, :] = tail.astype(BF)
    feats = came_ref[:, 0:each, :].reshape(reqs, uf)
    top = reqs // 2
    share_ref[0:top, 0:uf] = feats[0:top]
    share_ref[0:top, uf:] = feats[top:]
    share_ref[top:, :] = acc_t[...].astype(BF)


def rank(factor, slots, users, items, counts, came, iw, weight):
    width, cands = items.shape
    reqs = users.shape[1]
    hi_units = iw.shape[1]
    rows = counts.shape[0]
    shards = came.shape[0]
    each = reqs // shards
    return pl.pallas_call(
        lambda *refs: rank_kernel(factor, slots, *refs),
        out_shape=(
            jax.ShapeDtypeStruct((shards, 2 * each + 4, width), BF),
            jax.ShapeDtypeStruct((reqs // 2 + rows, width), BF),
        ),
        scratch_shapes=[
            pltpu.VMEM((reqs, width), F32),
            pltpu.VMEM((width, hi_units), F32),
            pltpu.VMEM((rows, width), F32),
            pltpu.VMEM((8, hi_units), F32),
            pltpu.VMEM((shards, width), F32),
        ],
        compiler_params=pltpu.CompilerParams(vmem_limit_bytes=16 << 20),
        cost_estimate=pl.CostEstimate(
            flops=2 * cands * width * (reqs * 2 + hi_units * 3 + rows),
            bytes_accessed=4 << 20,
            transcendentals=cands * hi_units,
        ),
        name="rank",
    )(users, items, counts, came, iw, weight)


def fold_kernel(back_ref, own_ref, part_ref, score_ref):
    shards, each, width = own_ref.shape
    slots = score_ref.shape[1]
    came = back_ref[:, 2 * each : 2 * each + 4, :].astype(F32)
    line = lax.broadcasted_iota(jnp.int32, came.shape, 1)
    three = jnp.sum(jnp.where(line == 2, came, 0.0), axis=1)
    src = lax.broadcasted_iota(jnp.int32, (width, slots), 0)
    dst = lax.broadcasted_iota(jnp.int32, (width, slots), 1)
    pick = jnp.where((src % slots == dst) & (src < 3 * slots), 1.0, 0.0)
    score_ref[...] = mm(three.astype(BF), pick.astype(BF))
    total = back_ref[0, 0 : 2 * each + 4, :].astype(F32)
    for n in range(1, back_ref.shape[0]):
        total = total + back_ref[n, 0 : 2 * each + 4, :].astype(F32)
    own_ref[...] = jnp.broadcast_to(total[0:each].astype(BF)[None], (shards, each, width))
    part_ref[...] = total[each:].astype(BF)


def fold(back, each, slots):
    shards, width = back.shape[0], back.shape[2]
    return pl.pallas_call(
        fold_kernel,
        out_shape=(
            jax.ShapeDtypeStruct((shards, each, width), BF),
            jax.ShapeDtypeStruct((each + 4, width), BF),
            jax.ShapeDtypeStruct((shards, slots), F32),
        ),
        compiler_params=pltpu.CompilerParams(vmem_limit_bytes=6 << 20),
        name="fold",
    )(back)


def tie_kernel(p0, pa, pb, pc, t0, ta, tb, tc, after_ref, inter_ref, out_ref, column_ref):
    shards, each, width = inter_ref.shape
    f = [x[...].astype(F32) for x in (p0, pa, pb, pc)]
    total = (f[0] + f[3]) + (f[1] + f[2])
    inter_ref[...] = jnp.broadcast_to(total[0:each].astype(BF)[None], (shards, each, width))
    out_ref[:, 0:width] = total[each : each + 1]
    out_ref[:, width:] = total[each + 1 : each + 2]
    t = [x[...].astype(F32) for x in (t0, ta, tb, tc)]
    column_ref[...] = ((t[0] + t[3]) + (t[1] + t[2])).astype(BF)


def tie(parts, shares, after, shards, each):
    width = parts[0].shape[1]
    rows = shares[0].shape[0] // 2
    lower = pl.BlockSpec((rows, width), lambda i: (1, 0))
    return pl.pallas_call(
        tie_kernel,
        grid=(1,),
        in_specs=[pl.BlockSpec(parts[0].shape, lambda i: (0, 0))] * 4
        + [lower] * 4
        + [pl.BlockSpec(memory_space=pl.ANY)],
        out_specs=(
            pl.BlockSpec((shards, each, width), lambda i: (0, 0, 0)),
            pl.BlockSpec((1, 2 * width), lambda i: (0, 0)),
            pl.BlockSpec((rows, width), lambda i: (0, 0)),
        ),
        out_shape=(
            jax.ShapeDtypeStruct((shards, each, width), BF),
            jax.ShapeDtypeStruct((1, 2 * width), F32),
            jax.ShapeDtypeStruct((rows, width), BF),
        ),
        compiler_params=pltpu.CompilerParams(vmem_limit_bytes=8 << 20),
        name="tie",
    )(*parts, *shares, after)


def own_kernel(d_ref, feats_ref, win_ref, wout_ref, gout_ref, gin_ref):
    feats = flat(feats_ref)
    d = flat(d_ref)
    hid, slope = hidden_of(feats, win_ref[...])
    gout_ref[...] = mm(hid, d)
    d_pre = (mm_nt(wout_ref[...], d) * slope).astype(BF)
    gin_ref[...] = mm(d_pre, feats).T


def dense_own(d, feats, win_t, tower_out, each):
    wide, width = tower_out.shape
    uf = win_t.shape[1]
    reqs = each * feats.shape[0]
    block = 1024
    return pl.pallas_call(
        own_kernel,
        grid=(wide // block,),
        in_specs=[
            feats_spec(d, each, width),
            feats_spec(feats, each, uf),
            pl.BlockSpec((block, uf), lambda i: (i, 0)),
            pl.BlockSpec((block, width), lambda i: (i, 0)),
        ],
        out_specs=(
            pl.BlockSpec((block, width), lambda i: (i, 0)),
            pl.BlockSpec((uf, block), lambda i: (0, i)),
        ),
        out_shape=(pltpu.HBM((wide, width), F32), pltpu.HBM((uf, wide), F32)),
        compiler_params=pltpu.CompilerParams(vmem_limit_bytes=28 << 20),
        cost_estimate=pl.CostEstimate(
            flops=2 * reqs * wide * (2 * width + 2 * uf),
            bytes_accessed=10 << 20,
            transcendentals=reqs * wide,
        ),
        name="dense_own",
    )(d, feats, hbm(win_t), hbm(tower_out))


def finish_half(out_a, out_b, in_a, in_b, gout_ref, gin_ref):
    gout_ref[...] = out_a[...].astype(F32) + out_b[...].astype(F32)
    gin_ref[...] = in_a[...].astype(F32) + in_b[...].astype(F32)


def far_kernel(count, finishing, *refs):
    d, feats = refs[0:count], refs[count : 2 * count]
    win_ref, wout_ref, old_out, old_in = refs[2 * count : 2 * count + 4]
    rest = refs[2 * count + 4 :]
    if finishing:
        finish_half(*rest[0:4], *rest[6:8])
        rest = rest[4:6]
    gout_ref, gin_ref = rest
    wout = wout_ref[...]
    win = win_ref[...]
    d_all = jnp.concatenate([x[...] for x in d], axis=0)
    feats_all = jnp.concatenate([flat(x) for x in feats], axis=0)
    reqs = d[0].shape[0]
    hids, pres = [], []
    for k in range(count):
        hid, slope = hidden_of(feats_all[k * reqs : (k + 1) * reqs], win)
        hids.append(hid)
        pres.append((mm_nt(wout, d_all[k * reqs : (k + 1) * reqs]) * slope).astype(BF))
    out = old_out[...] + mm(jnp.concatenate(hids, axis=1), d_all)
    back = mm(jnp.concatenate(pres, axis=1), feats_all)
    gout_ref[...] = out.astype(BF)
    gin_ref[...] = (back.T + old_in[...]).astype(BF)


def dense_far(d, feats, win_t, tower_out, before, first, units, pieces):
    wide, width = tower_out.shape
    reqs = d[0].shape[0]
    uf = win_t.shape[1]
    count = len(d)
    block = 512
    base = first // block
    out_spec = pl.BlockSpec((block, width), lambda i: (i, 0))
    in_spec = pl.BlockSpec((uf, block), lambda i: (0, i))
    return pl.pallas_call(
        lambda *refs: far_kernel(count, pieces is not None, *refs),
        grid=(units // block,),
        in_specs=[pl.BlockSpec((reqs, width), lambda i: (0, 0))] * count
        + [pl.BlockSpec((reqs // 2, 2 * uf), lambda i: (0, 0))] * count
        + [
            pl.BlockSpec((block, uf), lambda i: (base + i, 0)),
            pl.BlockSpec((block, width), lambda i: (base + i, 0)),
            pl.BlockSpec((block, width), lambda i: (base + i, 0)),
            pl.BlockSpec((uf, block), lambda i: (0, base + i)),
        ]
        + ([out_spec] * 2 + [in_spec] * 2 if pieces else []),
        out_specs=(out_spec, in_spec) * (2 if pieces else 1),
        out_shape=(
            jax.ShapeDtypeStruct((units, width), BF),
            jax.ShapeDtypeStruct((uf, units), BF),
        )
        + ((pltpu.HBM((wide, width), F32), pltpu.HBM((uf, wide), F32)) if pieces else ()),
        compiler_params=pltpu.CompilerParams(vmem_limit_bytes=36 << 20),
        cost_estimate=pl.CostEstimate(
            flops=2 * count * reqs * units * (2 * width + 2 * uf),
            bytes_accessed=10 << 20,
            transcendentals=count * reqs * units,
        ),
        name="dense_far",
    )(*[hbm(x) for x in (*d, *feats, win_t, tower_out, *before)], *(pieces or ()))


def finish_kernel(*refs):
    gout_ref, gin_ref, table_ref, inter_ref = refs[-4:]
    finish_half(*refs[0:4], gout_ref, gin_ref)
    table_ref[...] = refs[4][...].astype(F32) + refs[5][...].astype(F32)
    width = table_ref.shape[1]
    inter_ref[:, 0:width] = refs[6][...].astype(F32).reshape(inter_ref.shape[0], width)
    inter_ref[:, width:] = refs[7][...].astype(F32).reshape(inter_ref.shape[0], width)


def finish(pieces, column, other, inter, before, first):
    units, width = pieces[0].shape
    uf = pieces[2].shape[0]
    wide = before[0].shape[0]
    shards, each, _ = inter.shape
    block = 512
    base = first // block
    steps = units // block
    part = column.shape[0] // steps
    near = shards // 2 // steps
    spec_o = pl.BlockSpec((block, width), lambda i: (i, 0))
    spec_i = pl.BlockSpec((uf, block), lambda i: (0, i))
    spec_t = pl.BlockSpec((part, width), lambda i: (i, 0))
    return pl.pallas_call(
        finish_kernel,
        grid=(steps,),
        in_specs=[spec_o, spec_o, spec_i, spec_i, spec_t, spec_t]
        + [
            pl.BlockSpec((near, each, width), lambda i: (i, 0, 0)),
            pl.BlockSpec((near, each, width), lambda i: (steps + i, 0, 0)),
        ]
        + [pl.BlockSpec(memory_space=pl.ANY)] * 2,
        out_specs=(
            pl.BlockSpec((block, width), lambda i: (base + i, 0)),
            pl.BlockSpec((uf, block), lambda i: (0, base + i)),
            spec_t,
            pl.BlockSpec((near * each, 2 * width), lambda i: (i, 0)),
        ),
        out_shape=(
            pltpu.HBM((wide, width), F32),
            pltpu.HBM((uf, wide), F32),
            jax.ShapeDtypeStruct(column.shape, F32),
            jax.ShapeDtypeStruct((shards // 2 * each, 2 * width), F32),
        ),
        input_output_aliases={8: 0, 9: 1},
        compiler_params=pltpu.CompilerParams(vmem_limit_bytes=12 << 20),
        name="finish",
    )(*pieces, column, other, inter, inter, *before)


def pack_kernel(feats_ref, req_ref, lab_ref, live_ref, out_ref):
    shards, slots = req_ref.shape
    each, lanes = feats_ref.shape
    req = req_ref[...].astype(F32)
    high = jnp.floor(req * (1.0 / 16.0))
    lab = lab_ref[...]
    lab_hi = lab.astype(BF).astype(F32)
    lab_mid = (lab - lab_hi).astype(BF).astype(F32)
    eye = lax.broadcasted_iota(jnp.int32, (shards, shards), 0) == lax.broadcasted_iota(
        jnp.int32, (shards, shards), 1
    )
    live = jnp.sum(
        jnp.where(eye, live_ref[...].astype(F32), 0.0), axis=1, keepdims=True
    )
    rows = []
    for group in (
        (high, req - high * 16.0, lab_hi, lab_mid),
        (lab - lab_hi - lab_mid, jnp.broadcast_to(live, (shards, slots))),
    ):
        total = jnp.zeros((shards, lanes), F32)
        for k, v in enumerate(group):
            src = lax.broadcasted_iota(jnp.int32, (slots, lanes), 0) + k * slots
            dst = lax.broadcasted_iota(jnp.int32, (slots, lanes), 1)
            total = total + mm(v.astype(BF), jnp.where(src == dst, 1.0, 0.0).astype(BF))
        rows.append(total)
    line = lax.broadcasted_iota(jnp.int32, (shards, each, lanes), 1)
    facts = jnp.where(
        line == 0, rows[0][:, None, :], jnp.where(line == 1, rows[1][:, None, :], 0.0)
    )
    out_ref[:, 0:each, :] = jnp.broadcast_to(feats_ref[...][None], (shards, each, lanes))
    out_ref[:, each : 2 * each, :] = facts.astype(BF)


def pack(feats, req, lab, live):
    each, lanes = feats.shape
    shards = req.shape[0]
    return pl.pallas_call(
        pack_kernel,
        out_shape=jax.ShapeDtypeStruct((shards, 2 * each, lanes), BF),
        compiler_params=pltpu.CompilerParams(vmem_limit_bytes=16 << 20),
        name="pack",
    )(*[hbm(x) for x in (feats, req, lab, live)])


def body(
    user_feats, tower_in, tower_out, table, inter_weight, out_weight, ids, live, req_of, labels
):
    groups = lax.axis_size("grp")
    shards = lax.axis_size("tbl")
    slots = ids.shape[3]
    width = table.shape[1]
    each = user_feats.shape[0]
    reqs = each * shards
    chips = groups // 2

    def ring(turn, other):
        return [
            (y * 2 + c, ((y + turn) % chips) * 2 + (c + other) % 2)
            for y in range(chips)
            for c in range(2)
        ]

    def from_chips(x):
        return [lax.ppermute(x, "grp", ring(turn, 0)) for turn in (1, chips - 1, 2)]

    def swap(x):
        return lax.ppermute(x, "grp", ring(0, 1))

    def exchange(x):
        return lax.all_to_all(x, "tbl", split_axis=0, concat_axis=0, tiled=True)

    arrived = exchange(pack(user_feats, req_of[0], labels[0], live))
    ids_rows = jnp.transpose(ids[0], (1, 0, 2)).reshape(ids.shape[2], shards * slots)
    items, counts = pool(ids_rows, table)
    win_t = tower_in.T
    users = user_vectors(arrived, tower_in, tower_out, each)
    factor = 1.0 / math.sqrt(groups * shards * shards * slots)
    sent, share = rank(
        factor, slots, users, items, counts, arrived, inter_weight, out_weight[:, None]
    )
    back = exchange(sent)
    far = from_chips(share)
    own, part, scores = fold(back, each, slots)
    third = exchange(own)
    pair = (part.astype(F32) + swap(part).astype(F32)).astype(BF)
    parts = [pair] + from_chips(pair)
    d_far = from_chips(third.reshape(reqs, width))
    before = dense_own(third, arrived, win_t, tower_out, each)
    inter_part, grad_out, column = tie(parts, [share] + far, hbm(before[1]), shards, each)
    inter_all = exchange(inter_part)
    other = swap(column)
    units = tower_out.shape[0] // 2
    pieces = None
    for k in range(2):
        g_out, g_in, *first = dense_far(
            d_far, far, win_t, tower_out, before, k * units, units, pieces
        )
        pieces = (g_out, swap(g_out), g_in, swap(g_in))
    sums = finish(pieces, column, other, inter_all, first, units)
    return (scores[None], sums[1], sums[0], sums[3], grad_out.reshape(-1), sums[2])


def solution(mesh):
    placed = (
        P(("grp", "tbl"), None),
        P(),
        P(),
        P("tbl", None),
        P(),
        P(),
        P(("grp", "tbl"), None, None, None),
        P(("grp", "tbl"), None),
        P(("grp", "tbl"), None, None),
        P(("grp", "tbl"), None, None),
    )
    return jax.shard_map(
        body,
        mesh=mesh,
        in_specs=placed,
        out_specs=(P(("grp", "tbl"), None, None), P(), P(), P(), P(), P("tbl", None)),
        check_vma=False,
    )
```

```python
import math

import jax
import jax.numpy as jnp
from jax import lax
from jax.experimental import pallas as pl
from jax.experimental.pallas import tpu as pltpu
from jax.sharding import PartitionSpec as P


BF = jnp.bfloat16
F32 = jnp.float32


def mm(a, b):
    return jnp.dot(a, b, preferred_element_type=F32)


def mm_nt(a, b):
    return lax.dot_general(a, b, (((1,), (1,)), ((), ())), preferred_element_type=F32)


def pool_kernel(ids_ref, table_ref, items_ref, counts_ref):
    rows, cands = counts_ref.shape
    row = lax.broadcasted_iota(jnp.int32, (rows, cands), 0)
    total = jnp.zeros((rows, cands), F32)
    for b in range(ids_ref.shape[0]):
        total = total + jnp.where(row == ids_ref[b : b + 1, :], 1.0, 0.0)
    counts = total.astype(BF)
    counts_ref[...] = counts
    items_ref[...] = mm(table_ref[...].astype(F32).T.astype(BF), counts).astype(BF)


def pool(ids, table):
    cands = ids.shape[1]
    rows, width = table.shape
    return pl.pallas_call(
        pool_kernel,
        out_shape=(
            jax.ShapeDtypeStruct((width, cands), BF),
            jax.ShapeDtypeStruct((rows, cands), BF),
        ),
        compiler_params=pltpu.CompilerParams(vmem_limit_bytes=8 << 20),
        cost_estimate=pl.CostEstimate(
            flops=2 * cands * rows * width, bytes_accessed=2 << 20, transcendentals=0
        ),
        name="pool",
    )(ids, table)


def sigmoid(value):
    return 0.5 * jnp.tanh(0.5 * value) + 0.5


def hbm(array):
    return pltpu.with_memory_space_constraint(array, pltpu.HBM)


def flat(ref):
    value = ref[...]
    if len(value.shape) == 3:
        return value.reshape(value.shape[0] * value.shape[1], value.shape[2])
    half = value.shape[1] // 2
    return jnp.concatenate([value[:, :half], value[:, half:]], axis=0)


def feats_spec(array, each, uf):
    if len(array.shape) == 3:
        return pl.BlockSpec((array.shape[0], each, uf), lambda i: (0, 0, 0))
    return pl.BlockSpec((array.shape[0] // 2, 2 * uf), lambda i: (0, 0))


def users_kernel(feats_ref, win_ref, wout_ref, users_ref, acc):
    step = pl.program_id(0)
    half = mm(flat(feats_ref) * jnp.asarray(0.5, BF), win_ref[...])
    part = mm((half * jnp.tanh(half) + half).astype(BF), wout_ref[...])

    @pl.when(step == 0)
    def _():
        acc[...] = part

    @pl.when(step > 0)
    def _():
        acc[...] += part

    @pl.when(step == pl.num_programs(0) - 1)
    def _():
        users_ref[...] = acc[...].T.astype(BF)


def user_vectors(feats, tower_in, tower_out, each):
    wide, width = tower_out.shape
    uf = tower_in.shape[0]
    reqs = feats.shape[0] * each
    block = 2048
    return pl.pallas_call(
        users_kernel,
        grid=(wide // block,),
        in_specs=[
            feats_spec(feats, each, uf),
            pl.BlockSpec((uf, block), lambda i: (0, i)),
            pl.BlockSpec((block, width), lambda i: (i, 0)),
        ],
        out_specs=pl.BlockSpec((width, reqs), lambda i: (0, 0)),
        out_shape=jax.ShapeDtypeStruct((width, reqs), BF),
        scratch_shapes=[pltpu.VMEM((reqs, width), F32)],
        compiler_params=pltpu.CompilerParams(vmem_limit_bytes=16 << 20),
        cost_estimate=pl.CostEstimate(
            flops=2 * reqs * wide * (uf + width),
            bytes_accessed=4 << 20,
            transcendentals=reqs * wide,
        ),
        name="users",
    )(feats, hbm(tower_in), hbm(tower_out))


def hidden_of(feats, win):
    half = mm_nt(win, feats * jnp.asarray(0.5, BF))
    turn = jnp.tanh(half)
    hid = half * turn + half
    rest = 0.5 - 0.5 * turn
    return hid.astype(BF), (1.0 - rest) + hid * rest


def rank_kernel(
    factor, slots, users_ref, items_ref, counts_ref, came_ref, iw_ref, w_ref,
    sent_ref, share_ref, acc_u, acc_g, acc_t, acc_o, acc_s,
):
    cands = items_ref.shape[1]
    reqs = users_ref.shape[1]
    width, _ = iw_ref.shape
    step_c = 256
    iw = iw_ref[...]
    iw_t = (iw.astype(F32) * 0.5).T.astype(BF)
    weight = w_ref[...]
    users = users_ref[...]
    shards, _, uf = came_ref.shape
    each = reqs // shards
    near = step_c // slots
    came = came_ref[:, each : 2 * each, :].astype(F32)
    line = lax.broadcasted_iota(jnp.int32, came.shape, 1)
    facts = [jnp.sum(jnp.where(line == n, came, 0.0), axis=1) for n in range(2)]
    src = lax.broadcasted_iota(jnp.int32, (uf, step_c), 0)
    dst = lax.broadcasted_iota(jnp.int32, (uf, step_c), 1) % slots
    spread = [jnp.where(src == dst + n * slots, 1.0, 0.0).astype(BF) for n in range(4)]
    src = lax.broadcasted_iota(jnp.int32, (step_c, width), 0) % slots
    dst = lax.broadcasted_iota(jnp.int32, (step_c, width), 1)
    gather = [jnp.where(src + n * slots == dst, 1.0, 0.0).astype(BF) for n in range(3)]
    mine = (
        lax.broadcasted_iota(jnp.int32, (near, step_c), 0)
        == lax.broadcasted_iota(jnp.int32, (near, step_c), 1) // slots
    )
    slot = lax.broadcasted_iota(jnp.int32, (1, step_c), 1) % slots
    for k in range(cands // step_c):
        cut = slice(k * step_c, (k + 1) * step_c)
        meta = []
        for n in range(6):
            part = facts[n // 4][k * near : (k + 1) * near, :].astype(BF)
            wide_part = jnp.where(mine, mm(part, spread[n % 4]), 0.0)
            meta.append(jnp.sum(wide_part, axis=0, keepdims=True))
        request = (meta[0] * 16.0 + meta[1]).astype(jnp.int32)
        target = meta[2] + meta[3] + meta[4]
        live = meta[5]
        row = lax.broadcasted_iota(jnp.int32, (reqs, step_c), 0)
        pick = jnp.where(row == request, 1.0, 0.0).astype(BF)
        chosen = mm(users, pick)
        item = items_ref[:, cut].astype(F32)
        cross = (item * chosen).astype(BF)
        half = mm(iw_t, cross)
        turn = jnp.tanh(half)
        act = half * turn + half
        rest = 0.5 - 0.5 * turn
        score = jnp.sum(act * weight, axis=0, keepdims=True)
        s_hi = score.astype(BF).astype(F32)
        s_mid = (score - s_hi).astype(BF).astype(F32)
        row_out = jnp.zeros((near, width), F32)
        for n, v in enumerate((s_hi, s_mid, (score - s_hi) - s_mid)):
            row_out = row_out + mm(jnp.where(mine, v, 0.0).astype(BF), gather[n])
        acc_s[k * near : (k + 1) * near, :] = row_out
        grad = jnp.where(slot.astype(F32) < live, sigmoid(score) - target, 0.0) * factor
        dz = (grad * weight * ((1.0 - rest) + act * rest)).astype(BF)
        dcross = mm(iw, dz)
        d_item = (dcross * chosen).astype(BF)
        d_user = (dcross * item).astype(BF)
        terms = mm_nt(pick, d_user)
        g_in = mm_nt(cross, dz)
        g_t = mm_nt(counts_ref[:, cut], d_item)
        g_o = mm_nt(jnp.broadcast_to(grad, (8, step_c)), act)
        if k == 0:
            acc_u[...] = terms
            acc_g[...] = g_in
            acc_t[...] = g_t
            acc_o[...] = g_o
        else:
            acc_u[...] += terms
            acc_g[...] += g_in
            acc_t[...] += g_t
            acc_o[...] += g_o
    sent_ref[:, 0:each, :] = acc_u[...].astype(BF).reshape(shards, each, width)
    half = shards // 2
    sent_ref[0:half, each : 2 * each, :] = acc_g[:, 0:width].astype(BF).reshape(half, each, width)
    sent_ref[half:, each : 2 * each, :] = acc_g[:, width:].astype(BF).reshape(half, each, width)
    line = lax.broadcasted_iota(jnp.int32, (shards, 4, width), 1)
    tail = jnp.where(
        line == 0,
        acc_o[0:1, 0:width][None],
        jnp.where(
            line == 1,
            acc_o[0:1, width:][None],
            jnp.where(line == 2, acc_s[...][:, None, :], 0.0),
        ),
    )
    sent_ref[:, 2 * each : 2 * each + 4, :] = tail.astype(BF)
    feats = came_ref[:, 0:each, :].reshape(reqs, uf)
    top = reqs // 2
    share_ref[0:top, 0:uf] = feats[0:top]
    share_ref[0:top, uf:] = feats[top:]
    share_ref[top:, :] = acc_t[...].astype(BF)


def rank(factor, slots, users, items, counts, came, iw, weight):
    width, cands = items.shape
    reqs = users.shape[1]
    hi_units = iw.shape[1]
    rows = counts.shape[0]
    shards = came.shape[0]
    each = reqs // shards
    return pl.pallas_call(
        lambda *refs: rank_kernel(factor, slots, *refs),
        out_shape=(
            jax.ShapeDtypeStruct((shards, 2 * each + 4, width), BF),
            jax.ShapeDtypeStruct((reqs // 2 + rows, width), BF),
        ),
        scratch_shapes=[
            pltpu.VMEM((reqs, width), F32),
            pltpu.VMEM((width, hi_units), F32),
            pltpu.VMEM((rows, width), F32),
            pltpu.VMEM((8, hi_units), F32),
            pltpu.VMEM((shards, width), F32),
        ],
        compiler_params=pltpu.CompilerParams(vmem_limit_bytes=16 << 20),
        cost_estimate=pl.CostEstimate(
            flops=2 * cands * width * (reqs * 2 + hi_units * 3 + rows),
            bytes_accessed=4 << 20,
            transcendentals=cands * hi_units,
        ),
        name="rank",
    )(users, items, counts, came, iw, weight)


def fold_kernel(back_ref, own_ref, part_ref, score_ref):
    shards, each, width = own_ref.shape
    slots = score_ref.shape[1]
    came = back_ref[:, 2 * each : 2 * each + 4, :].astype(F32)
    line = lax.broadcasted_iota(jnp.int32, came.shape, 1)
    three = jnp.sum(jnp.where(line == 2, came, 0.0), axis=1)
    src = lax.broadcasted_iota(jnp.int32, (width, slots), 0)
    dst = lax.broadcasted_iota(jnp.int32, (width, slots), 1)
    pick = jnp.where((src % slots == dst) & (src < 3 * slots), 1.0, 0.0)
    score_ref[...] = mm(three.astype(BF), pick.astype(BF))
    total = back_ref[0, 0 : 2 * each + 4, :].astype(F32)
    for n in range(1, back_ref.shape[0]):
        total = total + back_ref[n, 0 : 2 * each + 4, :].astype(F32)
    own_ref[...] = jnp.broadcast_to(total[0:each].astype(BF)[None], (shards, each, width))
    part_ref[...] = total[each:].astype(BF)


def fold(back, each, slots):
    shards, width = back.shape[0], back.shape[2]
    return pl.pallas_call(
        fold_kernel,
        out_shape=(
            jax.ShapeDtypeStruct((shards, each, width), BF),
            jax.ShapeDtypeStruct((each + 4, width), BF),
            jax.ShapeDtypeStruct((shards, slots), F32),
        ),
        compiler_params=pltpu.CompilerParams(vmem_limit_bytes=6 << 20),
        name="fold",
    )(back)


def tie_kernel(p0, pa, pb, pc, t0, ta, tb, tc, after_ref, inter_ref, out_ref, column_ref):
    shards, each, width = inter_ref.shape
    f = [x[...].astype(F32) for x in (p0, pa, pb, pc)]
    total = (f[0] + f[3]) + (f[1] + f[2])
    inter_ref[...] = jnp.broadcast_to(total[0:each].astype(BF)[None], (shards, each, width))
    out_ref[:, 0:width] = total[each : each + 1]
    out_ref[:, width:] = total[each + 1 : each + 2]
    t = [x[...].astype(F32) for x in (t0, ta, tb, tc)]
    column_ref[...] = ((t[0] + t[3]) + (t[1] + t[2])).astype(BF)


def tie(parts, shares, after, shards, each):
    width = parts[0].shape[1]
    rows = shares[0].shape[0] // 2
    lower = pl.BlockSpec((rows, width), lambda i: (1, 0))
    return pl.pallas_call(
        tie_kernel,
        grid=(1,),
        in_specs=[pl.BlockSpec(parts[0].shape, lambda i: (0, 0))] * 4
        + [lower] * 4
        + [pl.BlockSpec(memory_space=pl.ANY)],
        out_specs=(
            pl.BlockSpec((shards, each, width), lambda i: (0, 0, 0)),
            pl.BlockSpec((1, 2 * width), lambda i: (0, 0)),
            pl.BlockSpec((rows, width), lambda i: (0, 0)),
        ),
        out_shape=(
            jax.ShapeDtypeStruct((shards, each, width), BF),
            jax.ShapeDtypeStruct((1, 2 * width), F32),
            jax.ShapeDtypeStruct((rows, width), BF),
        ),
        compiler_params=pltpu.CompilerParams(vmem_limit_bytes=8 << 20),
        name="tie",
    )(*parts, *shares, after)


def own_kernel(d_ref, feats_ref, win_ref, wout_ref, gout_ref, gin_ref):
    feats = flat(feats_ref)
    d = flat(d_ref)
    hid, slope = hidden_of(feats, win_ref[...])
    gout_ref[...] = mm(hid, d)
    d_pre = (mm_nt(wout_ref[...], d) * slope).astype(BF)
    gin_ref[...] = mm(d_pre, feats).T


def dense_own(d, feats, win_t, tower_out, each, first, units):
    width = tower_out.shape[1]
    uf = win_t.shape[1]
    reqs = each * feats.shape[0]
    block = 1024
    base = first // block
    return pl.pallas_call(
        own_kernel,
        grid=(units // block,),
        in_specs=[
            feats_spec(d, each, width),
            feats_spec(feats, each, uf),
            pl.BlockSpec((block, uf), lambda i: (base + i, 0)),
            pl.BlockSpec((block, width), lambda i: (base + i, 0)),
        ],
        out_specs=(
            pl.BlockSpec((block, width), lambda i: (i, 0)),
            pl.BlockSpec((uf, block), lambda i: (0, i)),
        ),
        out_shape=(pltpu.HBM((units, width), F32), pltpu.HBM((uf, units), F32)),
        compiler_params=pltpu.CompilerParams(vmem_limit_bytes=28 << 20),
        cost_estimate=pl.CostEstimate(
            flops=2 * reqs * units * (2 * width + 2 * uf),
            bytes_accessed=10 << 20,
            transcendentals=reqs * units,
        ),
        name="dense_own",
    )(d, feats, hbm(win_t), hbm(tower_out))


def finish_half(out_a, out_b, in_a, in_b, gout_ref, gin_ref):
    gout_ref[...] = out_a[...].astype(F32) + out_b[...].astype(F32)
    gin_ref[...] = in_a[...].astype(F32) + in_b[...].astype(F32)


def far_kernel(count, finishing, *refs):
    d, feats = refs[0:count], refs[count : 2 * count]
    win_ref, wout_ref, old_out, old_in = refs[2 * count : 2 * count + 4]
    rest = refs[2 * count + 4 :]
    if finishing:
        finish_half(*rest[0:4], *rest[6:8])
        rest = rest[4:6]
    gout_ref, gin_ref = rest
    wout = wout_ref[...]
    win = win_ref[...]
    d_all = jnp.concatenate([x[...] for x in d], axis=0)
    feats_all = jnp.concatenate([flat(x) for x in feats], axis=0)
    reqs = d[0].shape[0]
    hids, pres = [], []
    for k in range(count):
        hid, slope = hidden_of(feats_all[k * reqs : (k + 1) * reqs], win)
        hids.append(hid)
        pres.append((mm_nt(wout, d_all[k * reqs : (k + 1) * reqs]) * slope).astype(BF))
    out = old_out[...] + mm(jnp.concatenate(hids, axis=1), d_all)
    back = mm(jnp.concatenate(pres, axis=1), feats_all)
    gout_ref[...] = out.astype(BF)
    gin_ref[...] = (back.T + old_in[...]).astype(BF)


def dense_far(d, feats, win_t, tower_out, before, first, units, pieces):
    wide, width = tower_out.shape
    reqs = d[0].shape[0]
    uf = win_t.shape[1]
    count = len(d)
    block = 512
    base = first // block
    out_spec = pl.BlockSpec((block, width), lambda i: (i, 0))
    in_spec = pl.BlockSpec((uf, block), lambda i: (0, i))
    return pl.pallas_call(
        lambda *refs: far_kernel(count, pieces is not None, *refs),
        grid=(units // block,),
        in_specs=[pl.BlockSpec((reqs, width), lambda i: (0, 0))] * count
        + [pl.BlockSpec((reqs // 2, 2 * uf), lambda i: (0, 0))] * count
        + [
            pl.BlockSpec((block, uf), lambda i: (base + i, 0)),
            pl.BlockSpec((block, width), lambda i: (base + i, 0)),
            out_spec,
            in_spec,
        ]
        + ([out_spec] * 2 + [in_spec] * 2 if pieces else []),
        out_specs=(out_spec, in_spec) * (2 if pieces else 1),
        out_shape=(
            jax.ShapeDtypeStruct((units, width), BF),
            jax.ShapeDtypeStruct((uf, units), BF),
        )
        + ((pltpu.HBM((wide, width), F32), pltpu.HBM((uf, wide), F32)) if pieces else ()),
        compiler_params=pltpu.CompilerParams(vmem_limit_bytes=36 << 20),
        cost_estimate=pl.CostEstimate(
            flops=2 * count * reqs * units * (2 * width + 2 * uf),
            bytes_accessed=10 << 20,
            transcendentals=count * reqs * units,
        ),
        name="dense_far",
    )(*[hbm(x) for x in (*d, *feats, win_t, tower_out, *before)], *(pieces or ()))


def finish_kernel(*refs):
    gout_ref, gin_ref, table_ref, inter_ref = refs[-4:]
    finish_half(*refs[0:4], gout_ref, gin_ref)
    table_ref[...] = refs[4][...].astype(F32) + refs[5][...].astype(F32)
    width = table_ref.shape[1]
    inter_ref[:, 0:width] = refs[6][...].astype(F32).reshape(inter_ref.shape[0], width)
    inter_ref[:, width:] = refs[7][...].astype(F32).reshape(inter_ref.shape[0], width)


def finish(pieces, column, other, inter, before, first):
    units, width = pieces[0].shape
    uf = pieces[2].shape[0]
    wide = before[0].shape[0]
    shards, each, _ = inter.shape
    block = 512
    base = first // block
    steps = units // block
    part = column.shape[0] // steps
    near = shards // 2 // steps
    spec_o = pl.BlockSpec((block, width), lambda i: (i, 0))
    spec_i = pl.BlockSpec((uf, block), lambda i: (0, i))
    spec_t = pl.BlockSpec((part, width), lambda i: (i, 0))
    return pl.pallas_call(
        finish_kernel,
        grid=(steps,),
        in_specs=[spec_o, spec_o, spec_i, spec_i, spec_t, spec_t]
        + [
            pl.BlockSpec((near, each, width), lambda i: (i, 0, 0)),
            pl.BlockSpec((near, each, width), lambda i: (steps + i, 0, 0)),
        ]
        + [pl.BlockSpec(memory_space=pl.ANY)] * 2,
        out_specs=(
            pl.BlockSpec((block, width), lambda i: (base + i, 0)),
            pl.BlockSpec((uf, block), lambda i: (0, base + i)),
            spec_t,
            pl.BlockSpec((near * each, 2 * width), lambda i: (i, 0)),
        ),
        out_shape=(
            pltpu.HBM((wide, width), F32),
            pltpu.HBM((uf, wide), F32),
            jax.ShapeDtypeStruct(column.shape, F32),
            jax.ShapeDtypeStruct((shards // 2 * each, 2 * width), F32),
        ),
        input_output_aliases={8: 0, 9: 1},
        compiler_params=pltpu.CompilerParams(vmem_limit_bytes=12 << 20),
        name="finish",
    )(*pieces, hbm(column), hbm(other), inter, inter, *before)


def pack_kernel(feats_ref, req_ref, lab_ref, live_ref, out_ref):
    shards, slots = req_ref.shape
    each, lanes = feats_ref.shape
    req = req_ref[...].astype(F32)
    high = jnp.floor(req * (1.0 / 16.0))
    lab = lab_ref[...]
    lab_hi = lab.astype(BF).astype(F32)
    lab_mid = (lab - lab_hi).astype(BF).astype(F32)
    eye = lax.broadcasted_iota(jnp.int32, (shards, shards), 0) == lax.broadcasted_iota(
        jnp.int32, (shards, shards), 1
    )
    live = jnp.sum(
        jnp.where(eye, live_ref[...].astype(F32), 0.0), axis=1, keepdims=True
    )
    rows = []
    for group in (
        (high, req - high * 16.0, lab_hi, lab_mid),
        (lab - lab_hi - lab_mid, jnp.broadcast_to(live, (shards, slots))),
    ):
        total = jnp.zeros((shards, lanes), F32)
        for k, v in enumerate(group):
            src = lax.broadcasted_iota(jnp.int32, (slots, lanes), 0) + k * slots
            dst = lax.broadcasted_iota(jnp.int32, (slots, lanes), 1)
            total = total + mm(v.astype(BF), jnp.where(src == dst, 1.0, 0.0).astype(BF))
        rows.append(total)
    line = lax.broadcasted_iota(jnp.int32, (shards, each, lanes), 1)
    facts = jnp.where(
        line == 0, rows[0][:, None, :], jnp.where(line == 1, rows[1][:, None, :], 0.0)
    )
    out_ref[:, 0:each, :] = jnp.broadcast_to(feats_ref[...][None], (shards, each, lanes))
    out_ref[:, each : 2 * each, :] = facts.astype(BF)


def pack(feats, req, lab, live):
    each, lanes = feats.shape
    shards = req.shape[0]
    return pl.pallas_call(
        pack_kernel,
        out_shape=jax.ShapeDtypeStruct((shards, 2 * each, lanes), BF),
        compiler_params=pltpu.CompilerParams(vmem_limit_bytes=16 << 20),
        name="pack",
    )(*[hbm(x) for x in (feats, req, lab, live)])


def body(
    user_feats, tower_in, tower_out, table, inter_weight, out_weight, ids, live, req_of, labels
):
    groups = lax.axis_size("grp")
    shards = lax.axis_size("tbl")
    slots = ids.shape[3]
    width = table.shape[1]
    each = user_feats.shape[0]
    reqs = each * shards
    chips = groups // 2

    def ring(turn, other):
        return [
            (y * 2 + c, ((y + turn) % chips) * 2 + (c + other) % 2)
            for y in range(chips)
            for c in range(2)
        ]

    def from_chips(x):
        return [lax.ppermute(x, "grp", ring(turn, 0)) for turn in (1, chips - 1, 2)]

    def swap(x):
        return lax.ppermute(x, "grp", ring(0, 1))

    def exchange(x):
        return lax.all_to_all(x, "tbl", split_axis=0, concat_axis=0, tiled=True)

    arrived = exchange(pack(user_feats, req_of[0], labels[0], live))
    ids_rows = jnp.transpose(ids[0], (1, 0, 2)).reshape(ids.shape[2], shards * slots)
    items, counts = pool(ids_rows, table)
    win_t = tower_in.T
    users = user_vectors(arrived, tower_in, tower_out, each)
    factor = 1.0 / math.sqrt(groups * shards * shards * slots)
    sent, share = rank(
        factor, slots, users, items, counts, arrived, inter_weight, out_weight[:, None]
    )
    back = exchange(sent)
    far = from_chips(share)
    own, part, scores = fold(back, each, slots)
    third = exchange(own)
    pair = (part.astype(F32) + swap(part).astype(F32)).astype(BF)
    parts = [pair] + from_chips(pair)
    d_far = from_chips(third.reshape(reqs, width))
    units = tower_out.shape[0] // 2
    before = []
    for k in range(2):
        before.append(dense_own(third, arrived, win_t, tower_out, each, k * units, units))
    inter_part, grad_out, column = tie(parts, [share] + far, hbm(before[0][1]), shards, each)
    inter_all = exchange(inter_part)
    other = swap(column)
    pieces = None
    for k in range(2):
        g_out, g_in, *first = dense_far(
            d_far, far, win_t, tower_out, before[k], k * units, units, pieces
        )
        pieces = (g_out, swap(g_out), g_in, swap(g_in))
    sums = finish(pieces, column, other, inter_all, first, units)
    return (scores[None], sums[1], sums[0], sums[3], grad_out.reshape(-1), sums[2])


def solution(mesh):
    placed = (
        P(("grp", "tbl"), None),
        P(),
        P(),
        P("tbl", None),
        P(),
        P(),
        P(("grp", "tbl"), None, None, None),
        P(("grp", "tbl"), None),
        P(("grp", "tbl"), None, None),
        P(("grp", "tbl"), None, None),
    )
    return jax.shard_map(
        body,
        mesh=mesh,
        in_specs=placed,
        out_specs=(P(("grp", "tbl"), None, None), P(), P(), P(), P(), P("tbl", None)),
        check_vma=False,
    )
```

```python
import math

import jax
import jax.numpy as jnp
from jax import lax
from jax.experimental import pallas as pl
from jax.experimental.pallas import tpu as pltpu
from jax.sharding import PartitionSpec as P


BF = jnp.bfloat16
F32 = jnp.float32


def mm(a, b):
    return jnp.dot(a, b, preferred_element_type=F32)


def mm_nt(a, b):
    return lax.dot_general(a, b, (((1,), (1,)), ((), ())), preferred_element_type=F32)


def pool_kernel(ids_ref, table_ref, items_ref, counts_ref):
    rows, cands = counts_ref.shape
    row = lax.broadcasted_iota(jnp.int32, (rows, cands), 0)
    total = jnp.zeros((rows, cands), F32)
    for b in range(ids_ref.shape[0]):
        total = total + jnp.where(row == ids_ref[b : b + 1, :], 1.0, 0.0)
    counts = total.astype(BF)
    counts_ref[...] = counts
    items_ref[...] = mm(table_ref[...].astype(F32).T.astype(BF), counts).astype(BF)


def pool(ids, table):
    cands = ids.shape[1]
    rows, width = table.shape
    return pl.pallas_call(
        pool_kernel,
        out_shape=(
            jax.ShapeDtypeStruct((width, cands), BF),
            jax.ShapeDtypeStruct((rows, cands), BF),
        ),
        compiler_params=pltpu.CompilerParams(vmem_limit_bytes=8 << 20),
        cost_estimate=pl.CostEstimate(
            flops=2 * cands * rows * width, bytes_accessed=2 << 20, transcendentals=0
        ),
        name="pool",
    )(ids, table)


def sigmoid(value):
    return 0.5 * jnp.tanh(0.5 * value) + 0.5


def hbm(array):
    return pltpu.with_memory_space_constraint(array, pltpu.HBM)


def flat(ref):
    value = ref[...]
    if len(value.shape) == 3:
        return value.reshape(value.shape[0] * value.shape[1], value.shape[2])
    half = value.shape[1] // 2
    return jnp.concatenate([value[:, :half], value[:, half:]], axis=0)


def feats_spec(array, each, uf):
    if len(array.shape) == 3:
        return pl.BlockSpec((array.shape[0], each, uf), lambda i: (0, 0, 0))
    return pl.BlockSpec((array.shape[0] // 2, 2 * uf), lambda i: (0, 0))


def users_kernel(feats_ref, win_ref, wout_ref, users_ref, acc):
    step = pl.program_id(0)
    half = mm(flat(feats_ref) * jnp.asarray(0.5, BF), win_ref[...])
    part = mm((half * jnp.tanh(half) + half).astype(BF), wout_ref[...])

    @pl.when(step == 0)
    def _():
        acc[...] = part

    @pl.when(step > 0)
    def _():
        acc[...] += part

    @pl.when(step == pl.num_programs(0) - 1)
    def _():
        users_ref[...] = acc[...].T.astype(BF)


def user_vectors(feats, tower_in, tower_out, each):
    wide, width = tower_out.shape
    uf = tower_in.shape[0]
    reqs = feats.shape[0] * each
    block = 2048
    return pl.pallas_call(
        users_kernel,
        grid=(wide // block,),
        in_specs=[
            feats_spec(feats, each, uf),
            pl.BlockSpec((uf, block), lambda i: (0, i)),
            pl.BlockSpec((block, width), lambda i: (i, 0)),
        ],
        out_specs=pl.BlockSpec((width, reqs), lambda i: (0, 0)),
        out_shape=jax.ShapeDtypeStruct((width, reqs), BF),
        scratch_shapes=[pltpu.VMEM((reqs, width), F32)],
        compiler_params=pltpu.CompilerParams(vmem_limit_bytes=16 << 20),
        cost_estimate=pl.CostEstimate(
            flops=2 * reqs * wide * (uf + width),
            bytes_accessed=4 << 20,
            transcendentals=reqs * wide,
        ),
        name="users",
    )(feats, hbm(tower_in), hbm(tower_out))


def hidden_of(feats, win):
    half = mm_nt(win, feats * jnp.asarray(0.5, BF))
    turn = jnp.tanh(half)
    hid = half * turn + half
    rest = 0.5 - 0.5 * turn
    return hid.astype(BF), (1.0 - rest) + hid * rest


def rank_kernel(
    factor, slots, users_ref, items_ref, counts_ref, came_ref, iw_ref, w_ref,
    sent_ref, share_ref, acc_u, acc_g, acc_t, acc_o, acc_s,
):
    cands = items_ref.shape[1]
    reqs = users_ref.shape[1]
    width, _ = iw_ref.shape
    step_c = 256
    iw = iw_ref[...]
    iw_t = (iw.astype(F32) * 0.5).T.astype(BF)
    weight = w_ref[...]
    users = users_ref[...]
    shards, _, uf = came_ref.shape
    each = reqs // shards
    near = step_c // slots
    came = came_ref[:, each : 2 * each, :].astype(F32)
    line = lax.broadcasted_iota(jnp.int32, came.shape, 1)
    facts = [jnp.sum(jnp.where(line == n, came, 0.0), axis=1) for n in range(2)]
    src = lax.broadcasted_iota(jnp.int32, (uf, step_c), 0)
    dst = lax.broadcasted_iota(jnp.int32, (uf, step_c), 1) % slots
    spread = [jnp.where(src == dst + n * slots, 1.0, 0.0).astype(BF) for n in range(4)]
    src = lax.broadcasted_iota(jnp.int32, (step_c, width), 0) % slots
    dst = lax.broadcasted_iota(jnp.int32, (step_c, width), 1)
    gather = [jnp.where(src + n * slots == dst, 1.0, 0.0).astype(BF) for n in range(3)]
    mine = (
        lax.broadcasted_iota(jnp.int32, (near, step_c), 0)
        == lax.broadcasted_iota(jnp.int32, (near, step_c), 1) // slots
    )
    slot = lax.broadcasted_iota(jnp.int32, (1, step_c), 1) % slots
    for k in range(cands // step_c):
        cut = slice(k * step_c, (k + 1) * step_c)
        meta = []
        for n in range(6):
            part = facts[n // 4][k * near : (k + 1) * near, :].astype(BF)
            wide_part = jnp.where(mine, mm(part, spread[n % 4]), 0.0)
            meta.append(jnp.sum(wide_part, axis=0, keepdims=True))
        request = (meta[0] * 16.0 + meta[1]).astype(jnp.int32)
        target = meta[2] + meta[3] + meta[4]
        live = meta[5]
        row = lax.broadcasted_iota(jnp.int32, (reqs, step_c), 0)
        pick = jnp.where(row == request, 1.0, 0.0).astype(BF)
        chosen = mm(users, pick)
        item = items_ref[:, cut].astype(F32)
        cross = (item * chosen).astype(BF)
        half = mm(iw_t, cross)
        turn = jnp.tanh(half)
        act = half * turn + half
        rest = 0.5 - 0.5 * turn
        score = jnp.sum(act * weight, axis=0, keepdims=True)
        s_hi = score.astype(BF).astype(F32)
        s_mid = (score - s_hi).astype(BF).astype(F32)
        row_out = jnp.zeros((near, width), F32)
        for n, v in enumerate((s_hi, s_mid, (score - s_hi) - s_mid)):
            row_out = row_out + mm(jnp.where(mine, v, 0.0).astype(BF), gather[n])
        acc_s[k * near : (k + 1) * near, :] = row_out
        grad = jnp.where(slot.astype(F32) < live, sigmoid(score) - target, 0.0) * factor
        dz = (grad * weight * ((1.0 - rest) + act * rest)).astype(BF)
        dcross = mm(iw, dz)
        d_item = (dcross * chosen).astype(BF)
        d_user = (dcross * item).astype(BF)
        terms = mm_nt(pick, d_user)
        g_in = mm_nt(cross, dz)
        g_t = mm_nt(counts_ref[:, cut], d_item)
        g_o = mm_nt(jnp.broadcast_to(grad, (8, step_c)), act)
        if k == 0:
            acc_u[...] = terms
            acc_g[...] = g_in
            acc_t[...] = g_t
            acc_o[...] = g_o
        else:
            acc_u[...] += terms
            acc_g[...] += g_in
            acc_t[...] += g_t
            acc_o[...] += g_o
    sent_ref[:, 0:each, :] = acc_u[...].astype(BF).reshape(shards, each, width)
    half = shards // 2
    sent_ref[0:half, each : 2 * each, :] = acc_g[:, 0:width].astype(BF).reshape(half, each, width)
    sent_ref[half:, each : 2 * each, :] = acc_g[:, width:].astype(BF).reshape(half, each, width)
    line = lax.broadcasted_iota(jnp.int32, (shards, 4, width), 1)
    tail = jnp.where(
        line == 0,
        acc_o[0:1, 0:width][None],
        jnp.where(
            line == 1,
            acc_o[0:1, width:][None],
            jnp.where(line == 2, acc_s[...][:, None, :], 0.0),
        ),
    )
    sent_ref[:, 2 * each : 2 * each + 4, :] = tail.astype(BF)
    feats = came_ref[:, 0:each, :].reshape(reqs, uf)
    top = reqs // 2
    share_ref[0:top, 0:uf] = feats[0:top]
    share_ref[0:top, uf:] = feats[top:]
    share_ref[top:, :] = acc_t[...].astype(BF)


def rank(factor, slots, users, items, counts, came, iw, weight):
    width, cands = items.shape
    reqs = users.shape[1]
    hi_units = iw.shape[1]
    rows = counts.shape[0]
    shards = came.shape[0]
    each = reqs // shards
    return pl.pallas_call(
        lambda *refs: rank_kernel(factor, slots, *refs),
        out_shape=(
            jax.ShapeDtypeStruct((shards, 2 * each + 4, width), BF),
            jax.ShapeDtypeStruct((reqs // 2 + rows, width), BF),
        ),
        scratch_shapes=[
            pltpu.VMEM((reqs, width), F32),
            pltpu.VMEM((width, hi_units), F32),
            pltpu.VMEM((rows, width), F32),
            pltpu.VMEM((8, hi_units), F32),
            pltpu.VMEM((shards, width), F32),
        ],
        compiler_params=pltpu.CompilerParams(vmem_limit_bytes=16 << 20),
        cost_estimate=pl.CostEstimate(
            flops=2 * cands * width * (reqs * 2 + hi_units * 3 + rows),
            bytes_accessed=4 << 20,
            transcendentals=cands * hi_units,
        ),
        name="rank",
    )(users, items, counts, came, iw, weight)


def fold_kernel(back_ref, own_ref, part_ref, score_ref):
    shards, each, width = own_ref.shape
    slots = score_ref.shape[1]
    came = back_ref[:, 2 * each : 2 * each + 4, :].astype(F32)
    line = lax.broadcasted_iota(jnp.int32, came.shape, 1)
    three = jnp.sum(jnp.where(line == 2, came, 0.0), axis=1)
    src = lax.broadcasted_iota(jnp.int32, (width, slots), 0)
    dst = lax.broadcasted_iota(jnp.int32, (width, slots), 1)
    pick = jnp.where((src % slots == dst) & (src < 3 * slots), 1.0, 0.0)
    score_ref[...] = mm(three.astype(BF), pick.astype(BF))
    total = back_ref[0, 0 : 2 * each + 4, :].astype(F32)
    for n in range(1, back_ref.shape[0]):
        total = total + back_ref[n, 0 : 2 * each + 4, :].astype(F32)
    own_ref[...] = jnp.broadcast_to(total[0:each].astype(BF)[None], (shards, each, width))
    part_ref[...] = total[each:].astype(BF)


def fold(back, each, slots):
    shards, width = back.shape[0], back.shape[2]
    return pl.pallas_call(
        fold_kernel,
        out_shape=(
            jax.ShapeDtypeStruct((shards, each, width), BF),
            jax.ShapeDtypeStruct((each + 4, width), BF),
            jax.ShapeDtypeStruct((shards, slots), F32),
        ),
        compiler_params=pltpu.CompilerParams(vmem_limit_bytes=6 << 20),
        name="fold",
    )(back)


def tie_kernel(p0, pa, pb, pc, t0, ta, tb, tc, after_ref, inter_ref, out_ref, column_ref):
    shards, each, width = inter_ref.shape
    f = [x[...].astype(F32) for x in (p0, pa, pb, pc)]
    total = (f[0] + f[3]) + (f[1] + f[2])
    inter_ref[...] = jnp.broadcast_to(total[0:each].astype(BF)[None], (shards, each, width))
    out_ref[:, 0:width] = total[each : each + 1]
    out_ref[:, width:] = total[each + 1 : each + 2]
    t = [x[...].astype(F32) for x in (t0, ta, tb, tc)]
    column_ref[...] = ((t[0] + t[3]) + (t[1] + t[2])).astype(BF)


def tie(parts, shares, after, shards, each):
    width = parts[0].shape[1]
    rows = shares[0].shape[0] // 2
    lower = pl.BlockSpec((rows, width), lambda i: (1, 0))
    return pl.pallas_call(
        tie_kernel,
        grid=(1,),
        in_specs=[pl.BlockSpec(parts[0].shape, lambda i: (0, 0))] * 4
        + [lower] * 4
        + [pl.BlockSpec(memory_space=pl.ANY)],
        out_specs=(
            pl.BlockSpec((shards, each, width), lambda i: (0, 0, 0)),
            pl.BlockSpec((1, 2 * width), lambda i: (0, 0)),
            pl.BlockSpec((rows, width), lambda i: (0, 0)),
        ),
        out_shape=(
            jax.ShapeDtypeStruct((shards, each, width), BF),
            jax.ShapeDtypeStruct((1, 2 * width), F32),
            jax.ShapeDtypeStruct((rows, width), BF),
        ),
        compiler_params=pltpu.CompilerParams(vmem_limit_bytes=8 << 20),
        name="tie",
    )(*parts, *[hbm(x) for x in shares], hbm(after))


def own_kernel(d_ref, feats_ref, win_ref, wout_ref, gout_ref, gin_ref):
    feats = flat(feats_ref)
    d = flat(d_ref)
    hid, slope = hidden_of(feats, win_ref[...])
    gout_ref[...] = mm(hid, d)
    d_pre = (mm_nt(wout_ref[...], d) * slope).astype(BF)
    gin_ref[...] = mm(d_pre, feats).T


def dense_own(d, feats, win_t, tower_out, each):
    wide, width = tower_out.shape
    uf = win_t.shape[1]
    reqs = each * feats.shape[0]
    block = 1024
    return pl.pallas_call(
        own_kernel,
        grid=(wide // block,),
        in_specs=[
            feats_spec(d, each, width),
            feats_spec(feats, each, uf),
            pl.BlockSpec((block, uf), lambda i: (i, 0)),
            pl.BlockSpec((block, width), lambda i: (i, 0)),
        ],
        out_specs=(
            pl.BlockSpec((block, width), lambda i: (i, 0)),
            pl.BlockSpec((uf, block), lambda i: (0, i)),
        ),
        out_shape=(pltpu.HBM((wide, width), F32), pltpu.HBM((uf, wide), F32)),
        compiler_params=pltpu.CompilerParams(vmem_limit_bytes=28 << 20),
        cost_estimate=pl.CostEstimate(
            flops=2 * reqs * wide * (2 * width + 2 * uf),
            bytes_accessed=10 << 20,
            transcendentals=reqs * wide,
        ),
        name="dense_own",
    )(d, feats, hbm(win_t), hbm(tower_out))


def finish_half(out_a, out_b, in_a, in_b, gout_ref, gin_ref):
    gout_ref[...] = out_a[...].astype(F32) + out_b[...].astype(F32)
    gin_ref[...] = in_a[...].astype(F32) + in_b[...].astype(F32)


def far_kernel(count, finishing, *refs):
    d, feats = refs[0:count], refs[count : 2 * count]
    win_ref, wout_ref, old_out, old_in = refs[2 * count : 2 * count + 4]
    rest = refs[2 * count + 4 :]
    if finishing:
        finish_half(*rest[0:4], *rest[6:8])
        rest = rest[4:6]
    gout_ref, gin_ref = rest
    wout = wout_ref[...]
    win = win_ref[...]
    d_all = jnp.concatenate([x[...] for x in d], axis=0)
    feats_all = jnp.concatenate([flat(x) for x in feats], axis=0)
    reqs = d[0].shape[0]
    hids, pres = [], []
    for k in range(count):
        hid, slope = hidden_of(feats_all[k * reqs : (k + 1) * reqs], win)
        hids.append(hid)
        pres.append((mm_nt(wout, d_all[k * reqs : (k + 1) * reqs]) * slope).astype(BF))
    out = old_out[...] + mm(jnp.concatenate(hids, axis=1), d_all)
    back = mm(jnp.concatenate(pres, axis=1), feats_all)
    gout_ref[...] = out.astype(BF)
    gin_ref[...] = (back.T + old_in[...]).astype(BF)


def dense_far(d, feats, win_t, tower_out, before, first, units, pieces):
    wide, width = tower_out.shape
    reqs = d[0].shape[0]
    uf = win_t.shape[1]
    count = len(d)
    block = 512
    base = first // block
    out_spec = pl.BlockSpec((block, width), lambda i: (i, 0))
    in_spec = pl.BlockSpec((uf, block), lambda i: (0, i))
    return pl.pallas_call(
        lambda *refs: far_kernel(count, pieces is not None, *refs),
        grid=(units // block,),
        in_specs=[pl.BlockSpec((reqs, width), lambda i: (0, 0))] * count
        + [pl.BlockSpec((reqs // 2, 2 * uf), lambda i: (0, 0))] * count
        + [
            pl.BlockSpec((block, uf), lambda i: (base + i, 0)),
            pl.BlockSpec((block, width), lambda i: (base + i, 0)),
            pl.BlockSpec((block, width), lambda i: (base + i, 0)),
            pl.BlockSpec((uf, block), lambda i: (0, base + i)),
        ]
        + ([out_spec] * 2 + [in_spec] * 2 if pieces else []),
        out_specs=(out_spec, in_spec) * (2 if pieces else 1),
        out_shape=(
            (jax.ShapeDtypeStruct if pieces else pltpu.HBM)((units, width), BF),
            (jax.ShapeDtypeStruct if pieces else pltpu.HBM)((uf, units), BF),
        )
        + ((pltpu.HBM((wide, width), F32), pltpu.HBM((uf, wide), F32)) if pieces else ()),
        compiler_params=pltpu.CompilerParams(vmem_limit_bytes=36 << 20),
        cost_estimate=pl.CostEstimate(
            flops=2 * count * reqs * units * (2 * width + 2 * uf),
            bytes_accessed=10 << 20,
            transcendentals=count * reqs * units,
        ),
        name="dense_far",
    )(*[hbm(x) for x in (*d, *feats, win_t, tower_out, *before)], *(pieces or ()))


def finish_kernel(*refs):
    gout_ref, gin_ref, table_ref, inter_ref = refs[-4:]
    finish_half(*refs[0:4], gout_ref, gin_ref)
    table_ref[...] = refs[4][...].astype(F32) + refs[5][...].astype(F32)
    width = table_ref.shape[1]
    inter_ref[:, 0:width] = refs[6][...].astype(F32).reshape(inter_ref.shape[0], width)
    inter_ref[:, width:] = refs[7][...].astype(F32).reshape(inter_ref.shape[0], width)


def finish(pieces, column, other, inter, before, first):
    units, width = pieces[0].shape
    uf = pieces[2].shape[0]
    wide = before[0].shape[0]
    shards, each, _ = inter.shape
    block = 512
    base = first // block
    steps = units // block
    part = column.shape[0] // steps
    near = shards // 2 // steps
    spec_o = pl.BlockSpec((block, width), lambda i: (i, 0))
    spec_i = pl.BlockSpec((uf, block), lambda i: (0, i))
    spec_t = pl.BlockSpec((part, width), lambda i: (i, 0))
    return pl.pallas_call(
        finish_kernel,
        grid=(steps,),
        in_specs=[spec_o, spec_o, spec_i, spec_i, spec_t, spec_t]
        + [
            pl.BlockSpec((near, each, width), lambda i: (i, 0, 0)),
            pl.BlockSpec((near, each, width), lambda i: (steps + i, 0, 0)),
        ]
        + [pl.BlockSpec(memory_space=pl.ANY)] * 2,
        out_specs=(
            pl.BlockSpec((block, width), lambda i: (base + i, 0)),
            pl.BlockSpec((uf, block), lambda i: (0, base + i)),
            spec_t,
            pl.BlockSpec((near * each, 2 * width), lambda i: (i, 0)),
        ),
        out_shape=(
            pltpu.HBM((wide, width), F32),
            pltpu.HBM((uf, wide), F32),
            jax.ShapeDtypeStruct(column.shape, F32),
            jax.ShapeDtypeStruct((shards // 2 * each, 2 * width), F32),
        ),
        input_output_aliases={8: 0, 9: 1},
        compiler_params=pltpu.CompilerParams(vmem_limit_bytes=12 << 20),
        name="finish",
    )(*pieces, column, other, inter, inter, *before)


def pack_kernel(feats_ref, req_ref, lab_ref, live_ref, out_ref):
    shards, slots = req_ref.shape
    each, lanes = feats_ref.shape
    req = req_ref[...].astype(F32)
    high = jnp.floor(req * (1.0 / 16.0))
    lab = lab_ref[...]
    lab_hi = lab.astype(BF).astype(F32)
    lab_mid = (lab - lab_hi).astype(BF).astype(F32)
    eye = lax.broadcasted_iota(jnp.int32, (shards, shards), 0) == lax.broadcasted_iota(
        jnp.int32, (shards, shards), 1
    )
    live = jnp.sum(
        jnp.where(eye, live_ref[...].astype(F32), 0.0), axis=1, keepdims=True
    )
    rows = []
    for group in (
        (high, req - high * 16.0, lab_hi, lab_mid),
        (lab - lab_hi - lab_mid, jnp.broadcast_to(live, (shards, slots))),
    ):
        total = jnp.zeros((shards, lanes), F32)
        for k, v in enumerate(group):
            src = lax.broadcasted_iota(jnp.int32, (slots, lanes), 0) + k * slots
            dst = lax.broadcasted_iota(jnp.int32, (slots, lanes), 1)
            total = total + mm(v.astype(BF), jnp.where(src == dst, 1.0, 0.0).astype(BF))
        rows.append(total)
    line = lax.broadcasted_iota(jnp.int32, (shards, each, lanes), 1)
    facts = jnp.where(
        line == 0, rows[0][:, None, :], jnp.where(line == 1, rows[1][:, None, :], 0.0)
    )
    out_ref[:, 0:each, :] = jnp.broadcast_to(feats_ref[...][None], (shards, each, lanes))
    out_ref[:, each : 2 * each, :] = facts.astype(BF)


def pack(feats, req, lab, live):
    each, lanes = feats.shape
    shards = req.shape[0]
    return pl.pallas_call(
        pack_kernel,
        out_shape=jax.ShapeDtypeStruct((shards, 2 * each, lanes), BF),
        compiler_params=pltpu.CompilerParams(vmem_limit_bytes=16 << 20),
        name="pack",
    )(*[hbm(x) for x in (feats, req, lab, live)])


def body(
    user_feats, tower_in, tower_out, table, inter_weight, out_weight, ids, live, req_of, labels
):
    groups = lax.axis_size("grp")
    shards = lax.axis_size("tbl")
    slots = ids.shape[3]
    width = table.shape[1]
    each = user_feats.shape[0]
    reqs = each * shards
    chips = groups // 2

    def ring(turn, other):
        return [
            (y * 2 + c, ((y + turn) % chips) * 2 + (c + other) % 2)
            for y in range(chips)
            for c in range(2)
        ]

    def from_chips(x):
        return [lax.ppermute(x, "grp", ring(turn, 0)) for turn in (1, chips - 1, 2)]

    def swap(x):
        return lax.ppermute(x, "grp", ring(0, 1))

    def exchange(x):
        return lax.all_to_all(x, "tbl", split_axis=0, concat_axis=0, tiled=True)

    arrived = exchange(pack(user_feats, req_of[0], labels[0], live))
    ids_rows = jnp.transpose(ids[0], (1, 0, 2)).reshape(ids.shape[2], shards * slots)
    items, counts = pool(ids_rows, table)
    win_t = tower_in.T
    users = user_vectors(arrived, tower_in, tower_out, each)
    factor = 1.0 / math.sqrt(groups * shards * shards * slots)
    sent, share = rank(
        factor, slots, users, items, counts, arrived, inter_weight, out_weight[:, None]
    )
    back = exchange(sent)
    far = from_chips(share)
    own, part, scores = fold(back, each, slots)
    third = exchange(own)
    pair = (part.astype(F32) + swap(part).astype(F32)).astype(BF)
    parts = [pair] + from_chips(pair)
    d_far = from_chips(third.reshape(reqs, width))
    before = dense_own(third, arrived, win_t, tower_out, each)
    units = tower_out.shape[0] // 2
    pieces = None
    for k in range(2):
        g_out, g_in, *first = dense_far(
            d_far, far, win_t, tower_out, before, k * units, units, pieces
        )
        pieces = (g_out, swap(g_out), g_in, swap(g_in))
        if k == 0:
            inter_part, grad_out, column = tie(parts, [share] + far, g_in, shards, each)
            inter_all = exchange(inter_part)
            other = swap(column)
    sums = finish(pieces, column, other, inter_all, first, units)
    return (scores[None], sums[1], sums[0], sums[3], grad_out.reshape(-1), sums[2])


def solution(mesh):
    placed = (
        P(("grp", "tbl"), None),
        P(),
        P(),
        P("tbl", None),
        P(),
        P(),
        P(("grp", "tbl"), None, None, None),
        P(("grp", "tbl"), None),
        P(("grp", "tbl"), None, None),
        P(("grp", "tbl"), None, None),
    )
    return jax.shard_map(
        body,
        mesh=mesh,
        in_specs=placed,
        out_specs=(P(("grp", "tbl"), None, None), P(), P(), P(), P(), P("tbl", None)),
        check_vma=False,
    )
```
